256 devices in a mesh: req: 16 (over y_lo, z), tensor: 16 (over y_hi, x, core).
Axes of the slice: x: 4, y: 4 (y_hi: 2, y_lo: 2; y = y_hi * 2 + y_lo), z: 8, core: 2. Of those that a mesh axis runs over, the one named last changes fastest.
Arguments:
- activations: bfloat16 [8192, 8192], P(('req', 'tensor')), parts along dimension 0, may hold values from -6 to 6
- norm_gain: float32 [8192], replicated, may hold values from 0.1 to 1.9
- query_weight: bfloat16 [8192, 4096], P(None, 'tensor'), may hold values from -0.0625 to 0.0625
- keyvalue_weight: bfloat16 [8192, 2048], P(None, 'tensor'), may hold values from -0.0625 to 0.0625
- output_weight: bfloat16 [4096, 8192], P('tensor'), may hold values from -0.09375 to 0.09375
- page_pool: bfloat16 [2048, 128, 256], P(('req', 'tensor')), parts along dimension 0, may hold values from -320 to 320
- page_table: int32 [288, 8], P('req'), parts along dimension 0, may hold values from 0 to 15
- prefill_offsets: int32 [32], P('req'), parts along dimension 0, may hold values from 0 to 1024, as said below
- decode_lengths: int32 [256], P('req'), parts along dimension 0, may hold values from 1 to 1024, as said below
Outputs:
- block_output: bfloat16 [8192, 8192], P(('req', 'tensor')), parts along dimension 0
The draws below stay inside these ranges and needn't reach their ends.
There are 16 independent parts, one for each index of `req`. The reference program is written for one: setup_inputs(seed, part) draws one part's arguments, and reference() takes and returns one part's arrays. A program takes and returns all parts, laid end to end along the dimension named above; an argument that names none is the same for every part. Nothing has to cross between parts.
Inputs may be any that keep to these rules, and one draw needn't show every extreme that they name: `page_table`: pages may be shared between requests. `decode_lengths`: some decode request has exactly 1024 cached tokens. `prefill_offsets`: some stretch has exactly 1024 cached tokens before it.
All inputs are finite; a program needn't handle non-finite values.
Results may differ from the reference program's by a relative error of at most 0.0095.
The reference program's roundings to bfloat16 on the way (of `normed`, `queries`, `new_keys`, `new_values` and `attended`) count: a program that leaves them out, or rounds other values in their place, can miss the bound.
Values may be sent and summed in bfloat16 or wider, within the bound.
A program may use at most 128 MiB of HBM per device.

```python
import jax
import jax.numpy as jnp
from jax import lax

D = 8192
QH = 32
KVH = 8
HD = 128
PAGE = 128
MAXP = 8
POOL = 16
C = 248
DEC = 16
ROWS = 512


def draw_page_pool(key, part):
    first, second = jax.random.split(jax.random.fold_in(key, 11), 2)
    shape = (KVH * POOL, PAGE, HD)
    key_part = jnp.clip(jax.random.normal(first, shape, jnp.float32), -4.0, 4.0)
    value_part = jnp.clip(jax.random.normal(second, shape, jnp.float32), -4.0, 4.0)
    return jnp.concatenate([key_part, value_part], axis=-1).astype(jnp.bfloat16)


def draw_prefill_offsets(key, part):
    first, second = jax.random.split(jax.random.fold_in(key, 23))
    drawn = jax.random.randint(first, (2,), 0, MAXP * PAGE + 1)
    chosen = jax.random.randint(second, (), 0, 2)
    return jnp.where(jnp.arange(2) == chosen, MAXP * PAGE, drawn).astype(jnp.int32)


def draw_decode_lengths(key, part):
    first, second = jax.random.split(jax.random.fold_in(key, 37))
    drawn = jax.random.randint(first, (DEC,), 1, MAXP * PAGE + 1)
    chosen = jax.random.randint(second, (), 0, DEC)
    return jnp.where(jnp.arange(DEC) == chosen, MAXP * PAGE, drawn).astype(jnp.int32)


def set_ends(values, stream_key, smallest, high):
    extent = values.shape
    place = [jax.random.randint(jax.random.fold_in(stream_key, axis), (), 0, extent[axis]) for axis in range(len(extent))]
    values = values.at[tuple(place)].set(smallest)
    longest = extent.index(max(extent))
    place[longest] = (place[longest] + 1) % extent[longest]
    return values.at[tuple(place)].set(high)


def block_scale(own_key, dims, cuts, least, largest):
    def one(dim, parts):
        draws = jax.random.uniform(jax.random.fold_in(jax.random.fold_in(own_key, 6), dim), (parts,), jnp.float32, least / len(cuts), largest / len(cuts))
        return jnp.repeat(jnp.exp(draws), dims[dim] // parts).reshape((-1,) + (1,) * (len(dims) - dim - 1))

    level = one(*cuts[0])
    for cut in cuts[1:]:
        level = level * one(*cut)
    return level


def centred(stream_key, extent, spread, limit, cuts=(), kind=jnp.bfloat16):
    entries = jax.random.normal(stream_key, extent, jnp.float32) * spread
    if len(cuts) > 0:
        entries = block_scale(stream_key, extent, cuts, -0.22, 0.18) * entries
    return jnp.clip(entries, min=-limit, max=limit).astype(kind)


def setup_inputs(seed: int = 0, part: int = 0) -> dict:
    key_of = jax.random.split(jax.random.key(seed), 10)
    part_keys = jax.random.split(jax.random.fold_in(key_of[9], part), 10)
    activations = centred(part_keys[0], (ROWS, D), 1.0, 6.0, ((0, 16),))
    norm_gain = jnp.clip(1.0 + 0.18 * jax.random.normal(key_of[1], (D,), jnp.float32), 0.1, 1.9)
    query_weight = centred(key_of[2], (D, QH * HD), D ** -0.5, 0.0625, ((1, 16),))
    keyvalue_weight = centred(key_of[3], (D, 2 * KVH * HD), D ** -0.5, 0.0625, ((1, 16),))
    output_weight = centred(key_of[4], (QH * HD, D), (QH * HD) ** -0.5, 0.09375, ((0, 16),))
    page_pool = draw_page_pool(jax.random.fold_in(jax.random.fold_in(key_of[9], part), 71), part)
    page_table = set_ends(jax.random.randint(part_keys[6], (2 + DEC, MAXP), 0, POOL), jax.random.fold_in(part_keys[6], 1), 0, POOL - 1).astype(jnp.int32)
    prefill_offsets = draw_prefill_offsets(jax.random.fold_in(jax.random.fold_in(key_of[9], part), 71), part)
    decode_lengths = draw_decode_lengths(jax.random.fold_in(jax.random.fold_in(key_of[9], part), 71), part)
    return dict(activations=activations, norm_gain=norm_gain, query_weight=query_weight, keyvalue_weight=keyvalue_weight, output_weight=output_weight, page_pool=page_pool, page_table=page_table, prefill_offsets=prefill_offsets, decode_lengths=decode_lengths)


eps_norm = 1e-06
rope_base = 1000000.0
neg_big = -1e+30

def rotate(values, positions):
    half_dim = values.shape[-1] // 2
    frequency = rope_base ** (-2.0 * jnp.arange(half_dim, dtype=jnp.float32) / values.shape[-1])
    angles = positions.astype(jnp.float32)[:, None] * frequency[None, :]
    cosine = jnp.cos(angles)[:, None, :]
    sine_part = jnp.sin(angles)[:, None, :]
    first_half = values[..., :half_dim]
    second_half = values[..., half_dim:]
    return jnp.concatenate([first_half * cosine - second_half * sine_part, second_half * cosine + first_half * sine_part], axis=-1)

def attend(queries, key_rows, value_rows, visible):
    scores = jnp.einsum('rgd,sd->grs', queries.astype(jnp.float32), key_rows.astype(jnp.float32)) * HD ** (-0.5)
    scores = jnp.where(visible[None], scores, neg_big)
    highest = lax.optimization_barrier(jnp.max(scores, axis=-1, keepdims=True))
    weights = jnp.where(visible[None], jnp.exp(scores - highest), 0.0)
    totals = lax.optimization_barrier(jnp.sum(weights, axis=-1))
    rounded = lax.optimization_barrier(weights.astype(jnp.bfloat16)).astype(jnp.float32)
    blended = jnp.einsum('grs,sd->rgd', rounded, value_rows.astype(jnp.float32))
    return blended / jnp.transpose(totals)[..., None]

def reference(activations, norm_gain, query_weight, keyvalue_weight, output_weight, page_pool, page_table, prefill_offsets, decode_lengths):
    widened = activations.astype(jnp.float32)
    normed = (widened * lax.rsqrt(lax.optimization_barrier(jnp.mean(widened * widened, axis=-1, keepdims=True)) + eps_norm) * norm_gain).astype(jnp.bfloat16)
    inner = jnp.arange(C, dtype=jnp.int32)
    positions = jnp.concatenate([prefill_offsets[0] + inner, prefill_offsets[1] + inner, decode_lengths]).astype(jnp.int32)
    queries = rotate(jnp.dot(normed, query_weight, preferred_element_type=jnp.float32).reshape(ROWS, QH, HD), positions).astype(jnp.bfloat16)
    projected = jnp.dot(normed, keyvalue_weight, preferred_element_type=jnp.float32).reshape(ROWS, KVH, 2, HD)
    new_keys = rotate(projected[:, :, 0], positions).astype(jnp.bfloat16)
    new_values = projected[:, :, 1].astype(jnp.bfloat16)
    pools = page_pool.reshape(KVH, POOL, PAGE, 2 * HD)
    group = QH // KVH
    grouped = jnp.transpose(queries.reshape(ROWS, KVH, group, HD), (1, 0, 2, 3))
    key_span = MAXP * PAGE
    slot_ids = jnp.arange(key_span, dtype=jnp.int32)

    def one_head(head_item):
        head_queries, head_keys, head_values, pool_head = head_item
        outputs = []
        for stretch_id in range(2):
            lower = stretch_id * C
            fetched = pool_head[page_table[stretch_id]].reshape(key_span, 2 * HD)
            key_rows = jnp.concatenate([fetched[:, :HD], head_keys[lower:lower + C]], axis=0)
            value_rows = jnp.concatenate([fetched[:, HD:], head_values[lower:lower + C]], axis=0)
            cache_seen = jnp.broadcast_to((slot_ids < prefill_offsets[stretch_id])[None, :], (C, key_span))
            visible = jnp.concatenate([cache_seen, inner[:, None] >= inner[None, :]], axis=1)
            outputs.append(attend(head_queries[lower:lower + C], key_rows, value_rows, visible))

        def decode_one(decode_item):
            query_row, key_new, value_new, table_row, length_one = decode_item
            fetched = pool_head[table_row].reshape(key_span, 2 * HD)
            key_rows = jnp.concatenate([fetched[:, :HD], key_new[None]], axis=0)
            value_rows = jnp.concatenate([fetched[:, HD:], value_new[None]], axis=0)
            visible = jnp.concatenate([slot_ids < length_one, jnp.ones((1,), dtype=bool)])[None]
            return attend(query_row[None], key_rows, value_rows, visible)[0]
        decoded = lax.map(decode_one, (head_queries[2 * C:], head_keys[2 * C:], head_values[2 * C:], page_table[2:], decode_lengths))
        return jnp.concatenate(outputs + [decoded], axis=0).astype(jnp.bfloat16)
    attended = lax.map(one_head, (grouped, jnp.transpose(new_keys, (1, 0, 2)), jnp.transpose(new_values, (1, 0, 2)), pools))
    attended = jnp.transpose(attended, (1, 0, 2, 3)).reshape(ROWS, QH * HD)
    summed = jnp.dot(attended, output_weight, preferred_element_type=jnp.float32)
    return summed.astype(jnp.bfloat16)
```

```python
import functools

import jax
import jax.numpy as jnp
import numpy as np
from jax import lax
from jax.experimental import pallas as pl
from jax.experimental.pallas import tpu as pltpu
from jax.sharding import PartitionSpec as P

HD = 128
C = 248
PAGE = 128
MAXP = 8
ROWS = 512
D = 8192
CW = 1024
NC = D // CW
CA = 640
eps_norm = 1e-06
rope_base = 1000000.0
neg_big = -1e30
MESH = pl.DeviceIdType.MESH
F32 = jnp.float32
BF16 = jnp.bfloat16
B_LO = 112
B_ROWS = 256 - B_LO
SPAN = MAXP * PAGE


def kernel(
    x_ref, gain_ref, freq_ref, wq_hbm, wkv_hbm, wo_hbm, pool_hbm, table_ref, off_ref, len_ref,
    out_ref,
    xg, w, wo, pool, kvc, acc, newkv, qa, qb, qd, trig, sa, sb, sd, pa, pb, pd, la, lb, cnt, att,
    pbuf, r_al, r_ar, r_l, r_r, r_y, s_y, s_al, s_ar, s_l, s_r,
    own_sem, ws_sem, wr_sem, ag_s, ag_r, kv_s, kv_r, rs_s, rs_r,
):
    req = lax.axis_index("req")
    me = lax.axis_index("tensor")
    h, x, c = me // 8, (me // 2) % 4, me % 2

    def dev(hh, xx, cc):
        return (req, hh * 8 + xx * 2 + cc)

    xr, xl, xo = lax.rem(x + 1, 4), lax.rem(x + 3, 4), lax.rem(x + 2, 4)
    core_dev, right, left, across = dev(h, x, 1 - c), dev(h, xr, c), dev(h, xl, c), dev(1 - h, x, c)

    def send(src, dst, ssem, rsem, to):
        return pltpu.make_async_remote_copy(
            src_ref=src, dst_ref=dst, send_sem=ssem, recv_sem=rsem, device_id=to, device_id_type=MESH
        )

    qcol = pl.multiple_of(c * 256, 256)
    kcol = pl.multiple_of(512 + c * 128, 128)
    orow = pl.multiple_of(c * 256, 256)
    prow = c * 8
    own = [
        pltpu.make_async_copy(pool_hbm, pool.at[pl.ds(prow, 8)], own_sem.at[0]),
        pltpu.make_async_copy(wq_hbm, w.at[:, pl.ds(qcol, 256)], own_sem.at[1]),
        pltpu.make_async_copy(wkv_hbm, w.at[:, pl.ds(kcol, 128)], own_sem.at[2]),
        pltpu.make_async_copy(wo_hbm, wo.at[pl.ds(orow, 256)], own_sem.at[3]),
    ]
    for copy in own:
        copy.start()

    barrier = pltpu.get_barrier_semaphore()
    for to in (core_dev, right, left, across):
        pl.semaphore_signal(barrier, inc=1, device_id=to, device_id_type=MESH)

    mine = pl.multiple_of((h * 4 + x) * 32, 32)
    total = jnp.zeros((32, 1), F32)
    for i in range(NC):
        v = x_ref[:, i * CW : (i + 1) * CW].astype(F32)
        total = total + jnp.sum(v * v, axis=1, keepdims=True)
    inv = lax.rsqrt(total * (1.0 / D) + eps_norm)
    for i in range(NC):
        v = x_ref[:, i * CW : (i + 1) * CW].astype(F32)
        xg[i, pl.ds(mine, 32), :] = (v * inv * gain_ref[:, i * CW : (i + 1) * CW]).astype(BF16)

    pl.semaphore_wait(barrier, 4)

    swap_pool = send(pool_hbm, pool.at[pl.ds(prow, 8)], ws_sem.at[0], wr_sem.at[0], core_dev)
    swap_wo = send(wo_hbm, wo.at[pl.ds(orow, 256)], ws_sem.at[1], wr_sem.at[1], core_dev)

    def swap_q(i):
        r = pl.ds(pl.multiple_of(i * CW, CW), CW)
        return send(wq_hbm.at[r], w.at[r, pl.ds(qcol, 256)], ws_sem.at[2 + i], wr_sem.at[2 + i], core_dev)

    def swap_kv(i):
        r = pl.ds(pl.multiple_of(i * CW, CW), CW)
        return send(
            wkv_hbm.at[r], w.at[r, pl.ds(kcol, 128)], ws_sem.at[2 + NC + i], wr_sem.at[2 + NC + i], core_dev
        )

    def block(hh, xx):
        return pl.multiple_of((hh * 4 + xx) * 32, 32)

    b_own, b_par = block(h, x), block(1 - h, x)
    b_l, b_r, b_o = block(h, xl), block(h, xr), block(h, xo)
    p_l, p_r = block(1 - h, xl), block(1 - h, xr)

    def part(k, i, row, n, lo, hi, to):
        ref = xg.at[i, pl.ds(pl.multiple_of(row, 16), n), lo:hi]
        return send(ref, ref, ag_s.at[i, k], ag_r.at[i, k], to)

    def gather(k, i):
        if k == 0:
            return part(k, i, b_own, 32, 0, CA, across)
        if k == 1:
            return part(k, i, b_own, 32, 0, CA, right)
        if k == 2:
            return part(k, i, b_own, 32, 0, CA, left)
        if k == 3:
            return part(k, i, b_par, 32, 0, CA, right)
        if k == 4:
            return part(k, i, b_par, 32, 0, CA, left)
        if k == 5:
            return part(k, i, b_l, 16, 0, CA, right)
        if k == 6:
            return part(k, i, b_r + 16, 16, 0, CA, left)
        if k == 7:
            return part(k, i, p_l, 16, 0, CA, right)
        if k == 8:
            return part(k, i, p_r + 16, 16, 0, CA, left)
        if k == 9:
            return part(k, i, b_own, 32, CA, CW, right)
        if k == 10:
            return part(k, i, b_own, 32, CA, CW, left)
        if k == 11:
            return part(k, i, b_own, 32, CA, CW, across)
        if k == 12:
            return part(k, i, b_l, 16, CA, CW, right)
        if k == 13:
            return part(k, i, b_r + 16, 16, CA, CW, left)
        if k == 14:
            return part(k, i, b_l, 32, CA, CW, across)
        if k == 15:
            return part(k, i, b_r, 32, CA, CW, across)
        return part(k, i, b_o, 32, CA, CW, across)

    swap_pool.start()
    acc[...] = jnp.zeros_like(acc)
    own[0].wait()
    own[1].wait()
    own[2].wait()

    def gather_step(s, carry):
        @pl.when(s < NC)
        def _():
            for k in (0, 1, 2, 9, 10, 11):
                gather(k, s).start()
            swap_q(s).start()
            swap_kv(s).start()

        @pl.when((s >= 1) & (s < NC + 1))
        def _():
            i = s - 1
            gather(0, i).wait_recv()
            gather(3, i).start()
            gather(4, i).start()
            gather(9, i).wait_recv()
            gather(12, i).start()
            gather(14, i).start()
            gather(10, i).wait_recv()
            gather(13, i).start()
            gather(15, i).start()
            gather(1, i).wait_recv()
            gather(5, i).start()
            gather(2, i).wait_recv()
            gather(6, i).start()

        @pl.when((s >= 2) & (s < NC + 2))
        def _():
            i = s - 2
            gather(12, i).wait_recv()
            gather(13, i).wait_recv()
            gather(16, i).start()
            gather(3, i).wait_recv()
            gather(7, i).start()
            gather(4, i).wait_recv()
            gather(8, i).start()

        @pl.when(s == 3)
        def _():
            prepare()

        @pl.when(s >= 3)
        def _():
            i = s - 3
            for k in (5, 6, 7, 8, 11, 14, 15, 16):
                gather(k, i).wait_recv()
            swap_q(i).wait_recv()
            swap_kv(i).wait_recv()
            r = pl.ds(pl.multiple_of(i * CW, CW), CW)
            acc[...] += jnp.dot(xg[i], w[r, :], preferred_element_type=F32)

        return carry

    def prepare():
        swap_pool.wait_recv()
        swap_wo.start()
        for st in range(2):
            for j in range(MAXP):
                kvc[st, j * PAGE : (j + 1) * PAGE, :] = pool[table_ref[st, j]]
        slot = lax.broadcasted_iota(jnp.int32, (16, 2048), 1)
        page, inside = slot // PAGE, slot % PAGE
        rid = lax.broadcasted_iota(jnp.int32, (16, 1), 0)
        length = jnp.zeros((16, 1), jnp.int32)
        for b in range(16):
            length = jnp.where(rid == b, len_ref[b], length)
        count = jnp.zeros((16, 2048), F32)
        for j in range(MAXP):
            named = jnp.zeros((16, 1), jnp.int32)
            for b in range(16):
                named = jnp.where(rid == b, table_ref[2 + b, j], named)
            seen = (page == named) & (inside + j * PAGE < length)
            count = count + jnp.where(seen, 1.0, 0.0)
        cnt[...] = count
        lr = lax.broadcasted_iota(jnp.int32, (256, 1), 0)
        g = ((lr // 32) * 2 + c) * 32 + lr % 32
        position = jnp.where(g < C, off_ref[0] + g, off_ref[1] + g - C)
        for b in range(16):
            position = jnp.where(g == 2 * C + b, len_ref[b], position)
        angle = position.astype(F32) * freq_ref[...]
        lane = lax.broadcasted_iota(jnp.int32, (256, HD), 1)
        trig[0] = jnp.cos(angle)
        trig[1] = jnp.where(lane < HD // 2, -jnp.sin(angle), jnp.sin(angle))

    lax.fori_loop(0, NC + 3, gather_step, 0)

    def rotated(col):
        v = acc[:, col : col + HD]
        return (v * trig[0] + pltpu.roll(v, HD // 2, 1) * trig[1]).astype(BF16)

    base = pl.multiple_of(c * 256, 256)
    newkv[pl.ds(base, 256), 0:HD] = rotated(512)
    newkv[pl.ds(base, 256), HD : 2 * HD] = acc[:, 640:768].astype(BF16)
    for n in range(4):
        q = rotated(n * HD)
        qa[n * 128 : (n + 1) * 128, :] = q[0:128]
        qb[n * B_ROWS : (n + 1) * B_ROWS, :] = q[B_LO:256]
        qd[n * 16 : (n + 1) * 16, :] = q[240:256]
        if n == 0:
            kv_part = newkv.at[pl.ds(base, 256)]
            swap_new = send(kv_part, kv_part, kv_s, kv_r, core_dev)
            swap_new.start()

    def nt(a, b):
        return lax.dot_general(a, b, (((1,), (1,)), ((), ())), preferred_element_type=F32)

    sa[:, 0:SPAN] = nt(qa[...], kvc[0, :, 0:HD])
    sb[:, 0:SPAN] = nt(qb[...], kvc[1, :, 0:HD])
    swap_new.wait_recv()
    sa[:, SPAN : SPAN + 128] = nt(qa[...], newkv[0:128, 0:HD])
    sa[:, SPAN + 128 : SPAN + 256] = nt(qa[...], newkv[256:384, 0:HD])
    sb[:, SPAN : SPAN + 384] = nt(qb[...], newkv[128:512, 0:HD])
    scale = HD ** (-0.5)

    def globals_of(lr):
        return ((lr // 32) * 2 + c) * 32 + lr % 32

    def key_globals(row):
        lr = row % 256
        return ((lr // 32) * 2 + row // 256) * 32 + lr % 32

    def softmax(s_ref, p_ref, l_ref, r0, n, q_glob, key_glob, floor, width, limit):
        rows = pl.ds(pl.multiple_of(r0, 16), n)
        slots = lax.broadcasted_iota(jnp.int32, (1, SPAN), 1)
        sc = jnp.where(slots < limit, s_ref[rows, 0:SPAN], neg_big)
        sn = jnp.where(
            (key_glob <= q_glob) & (key_glob >= floor), s_ref[rows, SPAN : SPAN + width], neg_big
        )
        m = jnp.maximum(jnp.max(sc, axis=1, keepdims=True), jnp.max(sn, axis=1, keepdims=True))
        ec = jnp.exp((sc - m) * scale)
        en = jnp.exp((sn - m) * scale)
        l_ref[rows, :] = jnp.broadcast_to(
            jnp.sum(ec, axis=1, keepdims=True) + jnp.sum(en, axis=1, keepdims=True), (n, HD)
        )
        p_ref[rows, 0:SPAN] = ec.astype(BF16)
        p_ref[rows, SPAN : SPAN + width] = en.astype(BF16)

    def soft_a(b, carry):
        r0 = b * 32
        lr = lax.rem(r0, 128) + lax.broadcasted_iota(jnp.int32, (32, 1), 0)
        k = lax.broadcasted_iota(jnp.int32, (1, 256), 1)
        kg = key_globals(jnp.where(k < 128, k, k + 128))
        kg = jnp.where(kg < C, kg, 2 * ROWS)
        softmax(sa, pa, la, r0, 32, globals_of(lr), kg, 0, 256, off_ref[0])
        return carry

    def soft_b(b, carry):
        r0 = b * 48
        lr = B_LO + lax.rem(r0, B_ROWS) + lax.broadcasted_iota(jnp.int32, (48, 1), 0)
        k = lax.broadcasted_iota(jnp.int32, (1, 384), 1)
        softmax(sb, pb, lb, r0, 48, globals_of(lr), key_globals(k + 128), C, 384, off_ref[1])
        return carry

    lax.fori_loop(0, 16, soft_a, 0)
    oa = jnp.dot(pa[:, 0:SPAN], kvc[0, :, HD : 2 * HD], preferred_element_type=F32)
    oa = oa + jnp.dot(pa[:, SPAN : SPAN + 128], newkv[0:128, HD : 2 * HD], preferred_element_type=F32)
    oa = oa + jnp.dot(pa[:, SPAN + 128 : SPAN + 256], newkv[256:384, HD : 2 * HD], preferred_element_type=F32)
    oa = (oa / la[...]).astype(BF16)
    for n in range(4):
        att[0:128, n * HD : (n + 1) * HD] = oa[n * 128 : (n + 1) * 128]
    lax.fori_loop(0, 12, soft_b, 0)
    ob = jnp.dot(pb[:, 0:SPAN], kvc[1, :, HD : 2 * HD], preferred_element_type=F32)
    ob = ob + jnp.dot(pb[:, SPAN : SPAN + 384], newkv[128:512, HD : 2 * HD], preferred_element_type=F32)
    ob = (ob / lb[...]).astype(BF16)
    near = lax.broadcasted_iota(jnp.int32, (16, 1), 0) >= 8 + 8 * (1 - c)
    for n in range(4):
        cols = slice(n * HD, (n + 1) * HD)
        att[128:256, cols] = ob[n * B_ROWS + 16 : (n + 1) * B_ROWS]
        att[B_LO:128, cols] = jnp.where(
            near, ob[n * B_ROWS : n * B_ROWS + 16].astype(F32), att[B_LO:128, cols].astype(F32)
        ).astype(BF16)

    @pl.when(c == 1)
    def _():
        for b in range(16):
            sd[:, b * 128 : (b + 1) * 128] = nt(qd[...], pool[b, :, 0:HD])
        self_s = nt(qd[...], newkv[496:512, 0:HD])
        kid = lax.broadcasted_iota(jnp.int32, (64, 16), 1)
        qid = lax.broadcasted_iota(jnp.int32, (64, 16), 0) % 16
        self_s = jnp.where(kid == qid, self_s, neg_big)
        for n in range(4):
            rows = slice(n * 16, (n + 1) * 16)
            own_s = self_s[n * 16 : (n + 1) * 16]
            count = cnt[...]
            s = jnp.where(count > 0.0, sd[rows, :], neg_big)
            m = jnp.maximum(jnp.max(s, axis=1, keepdims=True), jnp.max(own_s, axis=1, keepdims=True))
            e = count * jnp.exp((s - m) * scale)
            e_own = jnp.exp((own_s - m) * scale)
            tot = jnp.sum(e, axis=1, keepdims=True) + jnp.sum(e_own, axis=1, keepdims=True)
            pd[rows, :] = e.astype(BF16)
            o = jnp.dot(e_own.astype(BF16), newkv[496:512, HD : 2 * HD], preferred_element_type=F32)
            for b in range(16):
                o = o + jnp.dot(
                    pd[rows, b * 128 : (b + 1) * 128], pool[b, :, HD : 2 * HD], preferred_element_type=F32
                )
            att[240:256, n * HD : (n + 1) * HD] = (o / tot).astype(BF16)

    own[3].wait()
    swap_wo.wait_recv()

    def scatter(k, i):
        ss, rr = rs_s.at[i, k], rs_r.at[i, k]
        if k == 0:
            return send(pbuf.at[i, :, xo, 0:16, 0:CA], r_al.at[i], ss, rr, right)
        if k == 1:
            return send(pbuf.at[i, :, xo, 16:32, 0:CA], r_ar.at[i], ss, rr, left)
        if k == 2:
            return send(pbuf.at[i, :, xr, :, 0:CA], r_l.at[i], ss, rr, right)
        if k == 3:
            return send(pbuf.at[i, :, xl, :, 0:CA], r_r.at[i], ss, rr, left)
        if k == 4:
            return send(pbuf.at[i, 1 - h, x, :, 0:CA], r_y.at[i], ss, rr, across)
        if k == 5:
            return send(pbuf.at[i, 1 - h, :, :, CA:CW], s_y.at[i], ss, rr, across)
        if k == 6:
            return send(pbuf.at[i, h, xo, 0:16, CA:CW], s_al.at[i], ss, rr, right)
        if k == 7:
            return send(pbuf.at[i, h, xo, 16:32, CA:CW], s_ar.at[i], ss, rr, left)
        if k == 8:
            return send(pbuf.at[i, h, xr, :, CA:CW], s_l.at[i], ss, rr, right)
        return send(pbuf.at[i, h, xl, :, CA:CW], s_r.at[i], ss, rr, left)

    def f(v):
        return v.astype(F32)

    def scatter_step(s, carry):
        @pl.when(s < NC)
        def _():
            for b in range(CW // 256):
                col = pl.multiple_of(s * CW + b * 256, 256)
                prod = jnp.dot(att[...], wo[:, pl.ds(col, 256)], preferred_element_type=F32)
                pbuf[s, :, :, :, b * 256 : (b + 1) * 256] = prod.astype(BF16).reshape(2, 4, 32, 256)
            for k in (0, 1, 5):
                scatter(k, s).start()

        @pl.when((s >= 1) & (s < NC + 1))
        def _():
            i = s - 1
            scatter(0, i).wait_recv()
            pbuf[i, :, xr, 0:16, 0:CA] = (f(pbuf[i, :, xr, 0:16, 0:CA]) + f(r_al[i])).astype(BF16)
            scatter(1, i).wait_recv()
            pbuf[i, :, xl, 16:32, 0:CA] = (f(pbuf[i, :, xl, 16:32, 0:CA]) + f(r_ar[i])).astype(BF16)
            scatter(2, i).start()
            scatter(3, i).start()
            scatter(5, i).wait_recv()
            pbuf[i, h, :, :, CA:CW] = (f(pbuf[i, h, :, :, CA:CW]) + f(s_y[i])).astype(BF16)
            scatter(6, i).start()
            scatter(7, i).start()

        @pl.when((s >= 2) & (s < NC + 2))
        def _():
            i = s - 2
            scatter(2, i).wait_recv()
            scatter(3, i).wait_recv()
            pbuf[i, 1 - h, x, :, 0:CA] = (
                f(pbuf[i, 1 - h, x, :, 0:CA]) + f(r_l[i, 1 - h]) + f(r_r[i, 1 - h])
            ).astype(BF16)
            scatter(4, i).start()
            scatter(6, i).wait_recv()
            pbuf[i, h, xr, 0:16, CA:CW] = (f(pbuf[i, h, xr, 0:16, CA:CW]) + f(s_al[i])).astype(BF16)
            scatter(7, i).wait_recv()
            pbuf[i, h, xl, 16:32, CA:CW] = (f(pbuf[i, h, xl, 16:32, CA:CW]) + f(s_ar[i])).astype(BF16)
            scatter(8, i).start()
            scatter(9, i).start()

        @pl.when(s >= 3)
        def _():
            i = s - 3
            scatter(4, i).wait_recv()
            ca = pl.ds(pl.multiple_of(i * CW, 128), CA)
            cb = pl.ds(pl.multiple_of(i * CW + CA, 128), CW - CA)
            out_ref[:, ca] = (
                f(pbuf[i, h, x, :, 0:CA]) + f(r_l[i, h]) + f(r_r[i, h]) + f(r_y[i])
            ).astype(BF16)
            scatter(8, i).wait_recv()
            scatter(9, i).wait_recv()
            out_ref[:, cb] = (f(pbuf[i, h, x, :, CA:CW]) + f(s_l[i]) + f(s_r[i])).astype(BF16)

        return carry

    lax.fori_loop(0, NC + 3, scatter_step, 0)

    def drain(i, carry):
        for k in range(17):
            gather(k, i).wait_send()
        for k in range(10):
            scatter(k, i).wait_send()
        swap_q(i).wait_send()
        swap_kv(i).wait_send()
        return carry

    lax.fori_loop(0, NC, drain, 0)
    swap_pool.wait_send()
    swap_wo.wait_send()
    swap_new.wait_send()


def shards(x, gain, wq, wkv, wo, pool, table, offsets, lengths):
    half = np.arange(HD) % (HD // 2)
    freq = jnp.asarray((rope_base ** (-2.0 * half / HD)).astype(np.float32))[None]
    vmem = pl.BlockSpec(memory_space=pltpu.VMEM)
    smem = pl.BlockSpec(memory_space=pltpu.SMEM)
    anyw = pl.BlockSpec(memory_space=pl.ANY)
    cb = CW - CA
    dma = pltpu.SemaphoreType.DMA
    return pl.pallas_call(
        kernel,
        name="block",
        out_shape=jax.ShapeDtypeStruct((32, D), BF16),
        in_specs=[vmem, vmem, vmem, anyw, anyw, anyw, anyw, smem, smem, smem],
        out_specs=vmem,
        scratch_shapes=[
            pltpu.VMEM((NC, 256, CW), BF16),
            pltpu.VMEM((D, 768), BF16),
            pltpu.VMEM((512, D), BF16),
            pltpu.VMEM((16, PAGE, 2 * HD), BF16),
            pltpu.VMEM((2, SPAN, 2 * HD), BF16),
            pltpu.VMEM((256, 768), F32),
            pltpu.VMEM((512, 2 * HD), BF16),
            pltpu.VMEM((512, HD), BF16),
            pltpu.VMEM((4 * B_ROWS, HD), BF16),
            pltpu.VMEM((64, HD), BF16),
            pltpu.VMEM((2, 256, HD), F32),
            pltpu.VMEM((512, SPAN + 256), F32),
            pltpu.VMEM((4 * B_ROWS, SPAN + 384), F32),
            pltpu.VMEM((64, 2048), F32),
            pltpu.VMEM((512, SPAN + 256), BF16),
            pltpu.VMEM((4 * B_ROWS, SPAN + 384), BF16),
            pltpu.VMEM((64, 2048), BF16),
            pltpu.VMEM((512, HD), F32),
            pltpu.VMEM((4 * B_ROWS, HD), F32),
            pltpu.VMEM((16, 2048), F32),
            pltpu.VMEM((256, 512), BF16),
            pltpu.VMEM((NC, 2, 4, 32, CW), BF16),
            pltpu.VMEM((NC, 2, 16, CA), BF16),
            pltpu.VMEM((NC, 2, 16, CA), BF16),
            pltpu.VMEM((NC, 2, 32, CA), BF16),
            pltpu.VMEM((NC, 2, 32, CA), BF16),
            pltpu.VMEM((NC, 32, CA), BF16),
            pltpu.VMEM((NC, 4, 32, cb), BF16),
            pltpu.VMEM((NC, 16, cb), BF16),
            pltpu.VMEM((NC, 16, cb), BF16),
            pltpu.VMEM((NC, 32, cb), BF16),
            pltpu.VMEM((NC, 32, cb), BF16),
            dma((4,)),
            dma((2 + 2 * NC,)),
            dma((2 + 2 * NC,)),
            dma((NC, 17)),
            dma((NC, 17)),
            dma,
            dma,
            dma((NC, 10)),
            dma((NC, 10)),
        ],
        compiler_params=pltpu.CompilerParams(
            collective_id=0, has_side_effects=True, vmem_limit_bytes=60 * 1024 * 1024
        ),
    )(x, gain[None], freq, wq, wkv, wo, pool, table, offsets, lengths)


def solution(mesh):
    placed = (
        P(("req", "tensor"), None),
        P(),
        P(None, "tensor"),
        P(None, "tensor"),
        P("tensor", None),
        P(("req", "tensor"), None, None),
        P("req", None),
        P("req"),
        P("req"),
    )
    return jax.shard_map(
        shards, mesh=mesh, in_specs=placed, out_specs=P(("req", "tensor"), None), check_vma=False
    )
```

```python
import functools

import jax
import jax.numpy as jnp
import numpy as np
from jax import lax
from jax.experimental import pallas as pl
from jax.experimental.pallas import tpu as pltpu
from jax.sharding import PartitionSpec as P

HD = 128
C = 248
PAGE = 128
MAXP = 8
ROWS = 512
D = 8192
CW = 1024
NC = D // CW
CA = 640
eps_norm = 1e-06
rope_base = 1000000.0
neg_big = -1e30
MESH = pl.DeviceIdType.MESH
F32 = jnp.float32
BF16 = jnp.bfloat16
B_LO = 112
B_ROWS = 256 - B_LO
SPAN = MAXP * PAGE


def kernel(
    x_hbm, gain_ref, freq_ref, wq_hbm, wkv_hbm, wo_hbm, pool_hbm, table_hbm, off_ref, len_ref,
    out_ref,
    x_ref, table_ref, xg, w, wo, pool, kvc, acc, newkv, qa, qb, qd, trig, sa, sb, sd, pa, pb, pd, la, lb, cnt, att,
    pbuf, r_al, r_ar, r_l, r_r, r_y, s_y, s_al, s_ar, s_l, s_r,
    in_sem, own_sem, ws_sem, wr_sem, ag_s, ag_r, kv_s, kv_r, rs_s, rs_r,
):
    req = lax.axis_index("req")
    me = lax.axis_index("tensor")
    h, x, c = me // 8, (me // 2) % 4, me % 2

    def dev(hh, xx, cc):
        return (req, hh * 8 + xx * 2 + cc)

    xr, xl, xo = lax.rem(x + 1, 4), lax.rem(x + 3, 4), lax.rem(x + 2, 4)
    core_dev, right, left, across = dev(h, x, 1 - c), dev(h, xr, c), dev(h, xl, c), dev(1 - h, x, c)

    def send(src, dst, ssem, rsem, to):
        return pltpu.make_async_remote_copy(
            src_ref=src, dst_ref=dst, send_sem=ssem, recv_sem=rsem, device_id=to, device_id_type=MESH
        )

    barrier = pltpu.get_barrier_semaphore()
    for to in (core_dev, right, left, across):
        pl.semaphore_signal(barrier, inc=1, device_id=to, device_id_type=MESH)

    rows_in = pltpu.make_async_copy(x_hbm, x_ref, in_sem.at[0])
    table_in = pltpu.make_async_copy(table_hbm, table_ref, in_sem.at[1])
    rows_in.start()
    table_in.start()

    qcol = pl.multiple_of(c * 256, 256)
    kcol = pl.multiple_of(512 + c * 128, 128)
    orow = pl.multiple_of(c * 256, 256)
    prow = c * 8
    own = [
        pltpu.make_async_copy(pool_hbm, pool.at[pl.ds(prow, 8)], own_sem.at[0]),
        pltpu.make_async_copy(wq_hbm, w.at[:, pl.ds(qcol, 256)], own_sem.at[1]),
        pltpu.make_async_copy(wkv_hbm, w.at[:, pl.ds(kcol, 128)], own_sem.at[2]),
        pltpu.make_async_copy(wo_hbm, wo.at[pl.ds(orow, 256)], own_sem.at[3]),
    ]
    for copy in own:
        copy.start()

    mine = pl.multiple_of((h * 4 + x) * 32, 32)
    total = jnp.zeros((32, 1), F32)
    rows_in.wait()
    for i in range(NC):
        v = x_ref[:, i * CW : (i + 1) * CW].astype(F32)
        total = total + jnp.sum(v * v, axis=1, keepdims=True)
    inv = lax.rsqrt(total * (1.0 / D) + eps_norm)
    for i in range(NC):
        v = x_ref[:, i * CW : (i + 1) * CW].astype(F32)
        xg[i, pl.ds(mine, 32), :] = (v * inv * gain_ref[:, i * CW : (i + 1) * CW]).astype(BF16)

    pl.semaphore_wait(barrier, 4)

    swap_pool = send(pool_hbm, pool.at[pl.ds(prow, 8)], ws_sem.at[0], wr_sem.at[0], core_dev)
    swap_wo = send(wo_hbm, wo.at[pl.ds(orow, 256)], ws_sem.at[1], wr_sem.at[1], core_dev)

    def swap_q(i):
        r = pl.ds(pl.multiple_of(i * CW, CW), CW)
        return send(wq_hbm.at[r], w.at[r, pl.ds(qcol, 256)], ws_sem.at[2 + i], wr_sem.at[2 + i], core_dev)

    def swap_kv(i):
        r = pl.ds(pl.multiple_of(i * CW, CW), CW)
        return send(
            wkv_hbm.at[r], w.at[r, pl.ds(kcol, 128)], ws_sem.at[2 + NC + i], wr_sem.at[2 + NC + i], core_dev
        )

    def block(hh, xx):
        return pl.multiple_of((hh * 4 + xx) * 32, 32)

    b_own, b_par = block(h, x), block(1 - h, x)
    b_l, b_r, b_o = block(h, xl), block(h, xr), block(h, xo)
    p_l, p_r = block(1 - h, xl), block(1 - h, xr)

    def part(k, i, row, n, lo, hi, to):
        ref = xg.at[i, pl.ds(pl.multiple_of(row, 16), n), lo:hi]
        return send(ref, ref, ag_s.at[i, k], ag_r.at[i, k], to)

    def gather(k, i):
        if k == 0:
            return part(k, i, b_own, 32, 0, CA, across)
        if k == 1:
            return part(k, i, b_own, 32, 0, CA, right)
        if k == 2:
            return part(k, i, b_own, 32, 0, CA, left)
        if k == 3:
            return part(k, i, b_par, 32, 0, CA, right)
        if k == 4:
            return part(k, i, b_par, 32, 0, CA, left)
        if k == 5:
            return part(k, i, b_l, 16, 0, CA, right)
        if k == 6:
            return part(k, i, b_r + 16, 16, 0, CA, left)
        if k == 7:
            return part(k, i, p_l, 16, 0, CA, right)
        if k == 8:
            return part(k, i, p_r + 16, 16, 0, CA, left)
        if k == 9:
            return part(k, i, b_own, 32, CA, CW, right)
        if k == 10:
            return part(k, i, b_own, 32, CA, CW, left)
        if k == 11:
            return part(k, i, b_own, 32, CA, CW, across)
        if k == 12:
            return part(k, i, b_l, 16, CA, CW, right)
        if k == 13:
            return part(k, i, b_r + 16, 16, CA, CW, left)
        if k == 14:
            return part(k, i, b_l, 32, CA, CW, across)
        if k == 15:
            return part(k, i, b_r, 32, CA, CW, across)
        return part(k, i, b_o, 32, CA, CW, across)

    swap_pool.start()
    acc[...] = jnp.zeros_like(acc)

    def gather_step(s, carry):
        @pl.when(s < NC)
        def _():
            for k in (0, 1, 2, 9, 10, 11):
                gather(k, s).start()
            swap_q(s).start()
            swap_kv(s).start()

        @pl.when((s >= 2) & (s < NC + 2))
        def _():
            i = s - 2
            gather(0, i).wait_recv()
            gather(3, i).start()
            gather(4, i).start()
            gather(9, i).wait_recv()
            gather(12, i).start()
            gather(14, i).start()
            gather(10, i).wait_recv()
            gather(13, i).start()
            gather(15, i).start()
            gather(1, i).wait_recv()
            gather(5, i).start()
            gather(2, i).wait_recv()
            gather(6, i).start()

        @pl.when((s >= 4) & (s < NC + 4))
        def _():
            i = s - 4
            gather(12, i).wait_recv()
            gather(13, i).wait_recv()
            gather(16, i).start()
            gather(3, i).wait_recv()
            gather(7, i).start()
            gather(4, i).wait_recv()
            gather(8, i).start()

        @pl.when(s == 5)
        def _():
            prepare()

        @pl.when(s >= 6)
        def _():
            i = s - 6
            for k in (5, 6, 7, 8, 11, 14, 15, 16):
                gather(k, i).wait_recv()
            swap_q(i).wait_recv()
            swap_kv(i).wait_recv()
            r = pl.ds(pl.multiple_of(i * CW, CW), CW)
            acc[...] += jnp.dot(xg[i], w[r, :], preferred_element_type=F32)

        return carry

    def prepare():
        own[0].wait()
        own[1].wait()
        own[2].wait()
        table_in.wait()
        swap_pool.wait_recv()
        swap_wo.start()
        for st in range(2):
            for j in range(MAXP):
                kvc[st, j * PAGE : (j + 1) * PAGE, :] = pool[table_ref[j, st]]
        slot = lax.broadcasted_iota(jnp.int32, (16, 2048), 1)
        page, inside = slot // PAGE, slot % PAGE
        rid = lax.broadcasted_iota(jnp.int32, (16, 1), 0)
        length = jnp.zeros((16, 1), jnp.int32)
        for b in range(16):
            length = jnp.where(rid == b, len_ref[b], length)
        count = jnp.zeros((16, 2048), F32)
        for j in range(MAXP):
            named = jnp.zeros((16, 1), jnp.int32)
            for b in range(16):
                named = jnp.where(rid == b, table_ref[j, 2 + b], named)
            seen = (page == named) & (inside + j * PAGE < length)
            count = count + jnp.where(seen, 1.0, 0.0)
        cnt[...] = count
        lr = lax.broadcasted_iota(jnp.int32, (256, 1), 0)
        g = ((lr // 32) * 2 + c) * 32 + lr % 32
        position = jnp.where(g < C, off_ref[0] + g, off_ref[1] + g - C)
        for b in range(16):
            position = jnp.where(g == 2 * C + b, len_ref[b], position)
        angle = position.astype(F32) * freq_ref[...]
        lane = lax.broadcasted_iota(jnp.int32, (256, HD), 1)
        trig[0] = jnp.cos(angle)
        trig[1] = jnp.where(lane < HD // 2, -jnp.sin(angle), jnp.sin(angle))

    lax.fori_loop(0, NC + 6, gather_step, 0)

    def rotated(col):
        v = acc[:, col : col + HD]
        return (v * trig[0] + pltpu.roll(v, HD // 2, 1) * trig[1]).astype(BF16)

    base = pl.multiple_of(c * 256, 256)
    newkv[pl.ds(base, 256), 0:HD] = rotated(512)
    newkv[pl.ds(base, 256), HD : 2 * HD] = acc[:, 640:768].astype(BF16)
    for n in range(4):
        q = rotated(n * HD)
        qa[n * 128 : (n + 1) * 128, :] = q[0:128]
        qb[n * B_ROWS : (n + 1) * B_ROWS, :] = q[B_LO:256]
        qd[n * 16 : (n + 1) * 16, :] = q[240:256]
        if n == 0:
            kv_part = newkv.at[pl.ds(base, 256)]
            swap_new = send(kv_part, kv_part, kv_s, kv_r, core_dev)
            swap_new.start()

    def nt(a, b):
        return lax.dot_general(a, b, (((1,), (1,)), ((), ())), preferred_element_type=F32)

    sa[:, 0:SPAN] = nt(qa[...], kvc[0, :, 0:HD])
    sb[:, 0:SPAN] = nt(qb[...], kvc[1, :, 0:HD])
    swap_new.wait_recv()
    sa[:, SPAN : SPAN + 128] = nt(qa[...], newkv[0:128, 0:HD])
    sa[:, SPAN + 128 : SPAN + 256] = nt(qa[...], newkv[256:384, 0:HD])
    sb[:, SPAN : SPAN + 384] = nt(qb[...], newkv[128:512, 0:HD])
    scale = HD ** (-0.5)

    def globals_of(lr):
        return ((lr // 32) * 2 + c) * 32 + lr % 32

    def key_globals(row):
        lr = row % 256
        return ((lr // 32) * 2 + row // 256) * 32 + lr % 32

    def softmax(s_ref, p_ref, l_ref, r0, n, q_glob, key_glob, floor, width, limit):
        rows = pl.ds(pl.multiple_of(r0, 16), n)
        slots = lax.broadcasted_iota(jnp.int32, (1, SPAN), 1)
        sc = jnp.where(slots < limit, s_ref[rows, 0:SPAN], neg_big)
        sn = jnp.where(
            (key_glob <= q_glob) & (key_glob >= floor), s_ref[rows, SPAN : SPAN + width], neg_big
        )
        m = jnp.maximum(jnp.max(sc, axis=1, keepdims=True), jnp.max(sn, axis=1, keepdims=True))
        ec = jnp.exp((sc - m) * scale)
        en = jnp.exp((sn - m) * scale)
        l_ref[rows, :] = jnp.broadcast_to(
            jnp.sum(ec, axis=1, keepdims=True) + jnp.sum(en, axis=1, keepdims=True), (n, HD)
        )
        p_ref[rows, 0:SPAN] = ec.astype(BF16)
        p_ref[rows, SPAN : SPAN + width] = en.astype(BF16)

    def soft_a(b, carry):
        r0 = b * 32
        lr = lax.rem(r0, 128) + lax.broadcasted_iota(jnp.int32, (32, 1), 0)
        k = lax.broadcasted_iota(jnp.int32, (1, 256), 1)
        kg = key_globals(jnp.where(k < 128, k, k + 128))
        kg = jnp.where(kg < C, kg, 2 * ROWS)
        softmax(sa, pa, la, r0, 32, globals_of(lr), kg, 0, 256, off_ref[0])
        return carry

    def soft_b(b, carry):
        r0 = b * 48
        lr = B_LO + lax.rem(r0, B_ROWS) + lax.broadcasted_iota(jnp.int32, (48, 1), 0)
        k = lax.broadcasted_iota(jnp.int32, (1, 384), 1)
        softmax(sb, pb, lb, r0, 48, globals_of(lr), key_globals(k + 128), C, 384, off_ref[1])
        return carry

    lax.fori_loop(0, 16, soft_a, 0)
    oa = jnp.dot(pa[:, 0:SPAN], kvc[0, :, HD : 2 * HD], preferred_element_type=F32)
    oa = oa + jnp.dot(pa[:, SPAN : SPAN + 128], newkv[0:128, HD : 2 * HD], preferred_element_type=F32)
    oa = oa + jnp.dot(pa[:, SPAN + 128 : SPAN + 256], newkv[256:384, HD : 2 * HD], preferred_element_type=F32)
    oa = (oa / la[...]).astype(BF16)
    for n in range(4):
        att[0:128, n * HD : (n + 1) * HD] = oa[n * 128 : (n + 1) * 128]
    lax.fori_loop(0, 12, soft_b, 0)
    ob = jnp.dot(pb[:, 0:SPAN], kvc[1, :, HD : 2 * HD], preferred_element_type=F32)
    ob = ob + jnp.dot(pb[:, SPAN : SPAN + 384], newkv[128:512, HD : 2 * HD], preferred_element_type=F32)
    ob = (ob / lb[...]).astype(BF16)
    near = lax.broadcasted_iota(jnp.int32, (16, 1), 0) >= 8 + 8 * (1 - c)
    for n in range(4):
        cols = slice(n * HD, (n + 1) * HD)
        att[128:256, cols] = ob[n * B_ROWS + 16 : (n + 1) * B_ROWS]
        att[B_LO:128, cols] = jnp.where(
            near, ob[n * B_ROWS : n * B_ROWS + 16].astype(F32), att[B_LO:128, cols].astype(F32)
        ).astype(BF16)

    @pl.when(c == 1)
    def _():
        for b in range(16):
            sd[:, b * 128 : (b + 1) * 128] = nt(qd[...], pool[b, :, 0:HD])
        self_s = nt(qd[...], newkv[496:512, 0:HD])
        kid = lax.broadcasted_iota(jnp.int32, (64, 16), 1)
        qid = lax.broadcasted_iota(jnp.int32, (64, 16), 0) % 16
        self_s = jnp.where(kid == qid, self_s, neg_big)
        for n in range(4):
            rows = slice(n * 16, (n + 1) * 16)
            own_s = self_s[n * 16 : (n + 1) * 16]
            count = cnt[...]
            s = jnp.where(count > 0.0, sd[rows, :], neg_big)
            m = jnp.maximum(jnp.max(s, axis=1, keepdims=True), jnp.max(own_s, axis=1, keepdims=True))
            e = count * jnp.exp((s - m) * scale)
            e_own = jnp.exp((own_s - m) * scale)
            tot = jnp.sum(e, axis=1, keepdims=True) + jnp.sum(e_own, axis=1, keepdims=True)
            pd[rows, :] = e.astype(BF16)
            o = jnp.dot(e_own.astype(BF16), newkv[496:512, HD : 2 * HD], preferred_element_type=F32)
            for b in range(16):
                o = o + jnp.dot(
                    pd[rows, b * 128 : (b + 1) * 128], pool[b, :, HD : 2 * HD], preferred_element_type=F32
                )
            att[240:256, n * HD : (n + 1) * HD] = (o / tot).astype(BF16)

    own[3].wait()
    swap_wo.wait_recv()

    def scatter(k, i):
        ss, rr = rs_s.at[i, k], rs_r.at[i, k]
        if k == 0:
            return send(pbuf.at[i, :, xo, 0:16, 0:CA], r_al.at[i], ss, rr, right)
        if k == 1:
            return send(pbuf.at[i, :, xo, 16:32, 0:CA], r_ar.at[i], ss, rr, left)
        if k == 2:
            return send(pbuf.at[i, :, xr, :, 0:CA], r_l.at[i], ss, rr, right)
        if k == 3:
            return send(pbuf.at[i, :, xl, :, 0:CA], r_r.at[i], ss, rr, left)
        if k == 4:
            return send(pbuf.at[i, 1 - h, x, :, 0:CA], r_y.at[i], ss, rr, across)
        if k == 5:
            return send(pbuf.at[i, 1 - h, :, :, CA:CW], s_y.at[i], ss, rr, across)
        if k == 6:
            return send(pbuf.at[i, h, xo, 0:16, CA:CW], s_al.at[i], ss, rr, right)
        if k == 7:
            return send(pbuf.at[i, h, xo, 16:32, CA:CW], s_ar.at[i], ss, rr, left)
        if k == 8:
            return send(pbuf.at[i, h, xr, :, CA:CW], s_l.at[i], ss, rr, right)
        return send(pbuf.at[i, h, xl, :, CA:CW], s_r.at[i], ss, rr, left)

    def f(v):
        return v.astype(F32)

    def scatter_step(s, carry):
        @pl.when(s < NC)
        def _():
            for b in range(CW // 256):
                col = pl.multiple_of(s * CW + b * 256, 256)
                prod = jnp.dot(att[...], wo[:, pl.ds(col, 256)], preferred_element_type=F32)
                pbuf[s, :, :, :, b * 256 : (b + 1) * 256] = prod.astype(BF16).reshape(2, 4, 32, 256)
            for k in (0, 1, 5):
                scatter(k, s).start()

        @pl.when((s >= 2) & (s < NC + 2))
        def _():
            i = s - 2
            scatter(0, i).wait_recv()
            pbuf[i, :, xr, 0:16, 0:CA] = (f(pbuf[i, :, xr, 0:16, 0:CA]) + f(r_al[i])).astype(BF16)
            scatter(1, i).wait_recv()
            pbuf[i, :, xl, 16:32, 0:CA] = (f(pbuf[i, :, xl, 16:32, 0:CA]) + f(r_ar[i])).astype(BF16)
            scatter(2, i).start()
            scatter(3, i).start()
            scatter(5, i).wait_recv()
            pbuf[i, h, :, :, CA:CW] = (f(pbuf[i, h, :, :, CA:CW]) + f(s_y[i])).astype(BF16)
            scatter(6, i).start()
            scatter(7, i).start()

        @pl.when((s >= 4) & (s < NC + 4))
        def _():
            i = s - 4
            scatter(2, i).wait_recv()
            scatter(3, i).wait_recv()
            pbuf[i, 1 - h, x, :, 0:CA] = (
                f(pbuf[i, 1 - h, x, :, 0:CA]) + f(r_l[i, 1 - h]) + f(r_r[i, 1 - h])
            ).astype(BF16)
            scatter(4, i).start()
            scatter(6, i).wait_recv()
            pbuf[i, h, xr, 0:16, CA:CW] = (f(pbuf[i, h, xr, 0:16, CA:CW]) + f(s_al[i])).astype(BF16)
            scatter(7, i).wait_recv()
            pbuf[i, h, xl, 16:32, CA:CW] = (f(pbuf[i, h, xl, 16:32, CA:CW]) + f(s_ar[i])).astype(BF16)
            scatter(8, i).start()
            scatter(9, i).start()

        @pl.when(s >= 6)
        def _():
            i = s - 6
            scatter(4, i).wait_recv()
            ca = pl.ds(pl.multiple_of(i * CW, 128), CA)
            cb = pl.ds(pl.multiple_of(i * CW + CA, 128), CW - CA)
            out_ref[:, ca] = (
                f(pbuf[i, h, x, :, 0:CA]) + f(r_l[i, h]) + f(r_r[i, h]) + f(r_y[i])
            ).astype(BF16)
            scatter(8, i).wait_recv()
            scatter(9, i).wait_recv()
            out_ref[:, cb] = (f(pbuf[i, h, x, :, CA:CW]) + f(s_l[i]) + f(s_r[i])).astype(BF16)

        return carry

    lax.fori_loop(0, NC + 6, scatter_step, 0)

    def drain(i, carry):
        for k in range(17):
            gather(k, i).wait_send()
        for k in range(10):
            scatter(k, i).wait_send()
        swap_q(i).wait_send()
        swap_kv(i).wait_send()
        return carry

    lax.fori_loop(0, NC, drain, 0)
    swap_pool.wait_send()
    swap_wo.wait_send()
    swap_new.wait_send()


def shards(x, gain, wq, wkv, wo, pool, table, offsets, lengths):
    half = np.arange(HD) % (HD // 2)
    freq = jnp.asarray((rope_base ** (-2.0 * half / HD)).astype(np.float32))[None]
    vmem = pl.BlockSpec(memory_space=pltpu.VMEM)
    smem = pl.BlockSpec(memory_space=pltpu.SMEM)
    anyw = pl.BlockSpec(memory_space=pl.ANY)
    cb = CW - CA
    dma = pltpu.SemaphoreType.DMA
    return pl.pallas_call(
        kernel,
        name="block",
        out_shape=jax.ShapeDtypeStruct((32, D), BF16),
        in_specs=[anyw, vmem, vmem, anyw, anyw, anyw, anyw, anyw, smem, smem],
        out_specs=vmem,
        scratch_shapes=[
            pltpu.VMEM((32, D), BF16),
            pltpu.SMEM((MAXP, 18), jnp.int32),
            pltpu.VMEM((NC, 256, CW), BF16),
            pltpu.VMEM((D, 768), BF16),
            pltpu.VMEM((512, D), BF16),
            pltpu.VMEM((16, PAGE, 2 * HD), BF16),
            pltpu.VMEM((2, SPAN, 2 * HD), BF16),
            pltpu.VMEM((256, 768), F32),
            pltpu.VMEM((512, 2 * HD), BF16),
            pltpu.VMEM((512, HD), BF16),
            pltpu.VMEM((4 * B_ROWS, HD), BF16),
            pltpu.VMEM((64, HD), BF16),
            pltpu.VMEM((2, 256, HD), F32),
            pltpu.VMEM((512, SPAN + 256), F32),
            pltpu.VMEM((4 * B_ROWS, SPAN + 384), F32),
            pltpu.VMEM((64, 2048), F32),
            pltpu.VMEM((512, SPAN + 256), BF16),
            pltpu.VMEM((4 * B_ROWS, SPAN + 384), BF16),
            pltpu.VMEM((64, 2048), BF16),
            pltpu.VMEM((512, HD), F32),
            pltpu.VMEM((4 * B_ROWS, HD), F32),
            pltpu.VMEM((16, 2048), F32),
            pltpu.VMEM((256, 512), BF16),
            pltpu.VMEM((NC, 2, 4, 32, CW), BF16),
            pltpu.VMEM((NC, 2, 16, CA), BF16),
            pltpu.VMEM((NC, 2, 16, CA), BF16),
            pltpu.VMEM((NC, 2, 32, CA), BF16),
            pltpu.VMEM((NC, 2, 32, CA), BF16),
            pltpu.VMEM((NC, 32, CA), BF16),
            pltpu.VMEM((NC, 4, 32, cb), BF16),
            pltpu.VMEM((NC, 16, cb), BF16),
            pltpu.VMEM((NC, 16, cb), BF16),
            pltpu.VMEM((NC, 32, cb), BF16),
            pltpu.VMEM((NC, 32, cb), BF16),
            dma((2,)),
            dma((4,)),
            dma((2 + 2 * NC,)),
            dma((2 + 2 * NC,)),
            dma((NC, 17)),
            dma((NC, 17)),
            dma,
            dma,
            dma((NC, 10)),
            dma((NC, 10)),
        ],
        compiler_params=pltpu.CompilerParams(
            collective_id=0, has_side_effects=True, vmem_limit_bytes=60 * 1024 * 1024
        ),
    )(x, gain[None], freq, wq, wkv, wo, pool, table.T, offsets, lengths)


def solution(mesh):
    placed = (
        P(("req", "tensor"), None),
        P(),
        P(None, "tensor"),
        P(None, "tensor"),
        P("tensor", None),
        P(("req", "tensor"), None, None),
        P("req", None),
        P("req"),
        P("req"),
    )
    return jax.shard_map(
        shards, mesh=mesh, in_specs=placed, out_specs=P(("req", "tensor"), None), check_vma=False
    )
```

```python
import functools

import jax
import jax.numpy as jnp
import numpy as np
from jax import lax
from jax.experimental import pallas as pl
from jax.experimental.pallas import tpu as pltpu
from jax.sharding import PartitionSpec as P

HD = 128
C = 248
PAGE = 128
MAXP = 8
ROWS = 512
D = 8192
CW = 2048
NN = D // CW
NB = 2
NC = NB * NN
CA = 1152
AH = 640
BH = CA + 384
eps_norm = 1e-06
rope_base = 1000000.0
neg_big = -1e30
MESH = pl.DeviceIdType.MESH
F32 = jnp.float32
BF16 = jnp.bfloat16
B_LO = (64, 48)
SPAN = MAXP * PAGE


def kernel(
    x_hbm, gain_ref, freq_ref, wq_hbm, wkv_hbm, wo_hbm, pool_hbm, table_hbm, off_ref, len_ref,
    out_ref,
    x_ref, table_ref, xg, w, wo, pool, kvc, acc, newkv, qa, qb, qd, trig, sc_ref, sf_ref, sd, pc, pd,
    m_ref, l_ref, o_ref, cnt, att, pbuf, r_al, r_ar, r_l, r_r, r_y, s_y, s_al, s_ar, s_l, s_r,
    in_sem, own_sem, ws_sem, wr_sem, ag_s, ag_r, kv_s, kv_r, rs_s, rs_r,
):
    req = lax.axis_index("req")
    me = lax.axis_index("tensor")
    h, x, c = me // 8, (me // 2) % 4, me % 2

    def dev(hh, xx, cc):
        return (req, hh * 8 + xx * 2 + cc)

    xr, xl, xo = lax.rem(x + 1, 4), lax.rem(x + 3, 4), lax.rem(x + 2, 4)
    core_dev, right, left, across = dev(h, x, 1 - c), dev(h, xr, c), dev(h, xl, c), dev(1 - h, x, c)

    def send(src, dst, ssem, rsem, to):
        return pltpu.make_async_remote_copy(
            src_ref=src, dst_ref=dst, send_sem=ssem, recv_sem=rsem, device_id=to, device_id_type=MESH
        )

    barrier = pltpu.get_barrier_semaphore()
    for to in (core_dev, right, left, across):
        pl.semaphore_signal(barrier, inc=1, device_id=to, device_id_type=MESH)

    rows_in = pltpu.make_async_copy(x_hbm, x_ref, in_sem.at[0])
    table_in = pltpu.make_async_copy(table_hbm, table_ref, in_sem.at[1])
    rows_in.start()
    table_in.start()

    qcol = pl.multiple_of(c * 256, 256)
    kcol = pl.multiple_of(512 + c * 128, 128)
    orow = pl.multiple_of(c * 256, 256)
    prow = c * 8
    own = [
        pltpu.make_async_copy(pool_hbm, pool.at[pl.ds(prow, 8)], own_sem.at[0]),
        pltpu.make_async_copy(wq_hbm, w.at[:, pl.ds(qcol, 256)], own_sem.at[1]),
        pltpu.make_async_copy(wkv_hbm, w.at[:, pl.ds(kcol, 128)], own_sem.at[2]),
        pltpu.make_async_copy(wo_hbm, wo.at[pl.ds(orow, 256)], own_sem.at[3]),
    ]
    for copy in own:
        copy.start()

    mine = pl.multiple_of((h * 4 + x) * 16, 16)
    total = jnp.zeros((32, 1), F32)
    rows_in.wait()
    for i in range(NN):
        v = x_ref[:, i * CW : (i + 1) * CW].astype(F32)
        total = total + jnp.sum(v * v, axis=1, keepdims=True)
    inv = lax.rsqrt(total * (1.0 / D) + eps_norm)
    for i in range(NN):
        v = x_ref[:, i * CW : (i + 1) * CW].astype(F32)
        v = (v * inv * gain_ref[:, i * CW : (i + 1) * CW]).astype(BF16)
        for b in range(NB):
            xg[b * NN + i, pl.ds(mine, 16), :] = v[b * 16 : (b + 1) * 16]

    pl.semaphore_wait(barrier, 4)

    swap_pool = send(pool_hbm, pool.at[pl.ds(prow, 8)], ws_sem.at[0], wr_sem.at[0], core_dev)
    swap_wo = send(wo_hbm, wo.at[pl.ds(orow, 256)], ws_sem.at[1], wr_sem.at[1], core_dev)

    def swap_q(i):
        r = pl.ds(pl.multiple_of(i * CW, CW), CW)
        return send(wq_hbm.at[r], w.at[r, pl.ds(qcol, 256)], ws_sem.at[2 + i], wr_sem.at[2 + i], core_dev)

    def swap_kv(i):
        r = pl.ds(pl.multiple_of(i * CW, CW), CW)
        return send(
            wkv_hbm.at[r], w.at[r, pl.ds(kcol, 128)], ws_sem.at[2 + NN + i], wr_sem.at[2 + NN + i], core_dev
        )

    def block(hh, xx):
        return pl.multiple_of((hh * 4 + xx) * 16, 16)

    b_own, b_par = block(h, x), block(1 - h, x)
    b_l, b_r, b_o = block(h, xl), block(h, xr), block(h, xo)
    p_l, p_r = block(1 - h, xl), block(1 - h, xr)

    def gather(k, i):
        row, lo, hi, to = (
            (b_own, 0, CA, across),
            (b_own, 0, CA, right),
            (b_own, 0, CA, left),
            (b_par, 0, CA, right),
            (b_par, 0, CA, left),
            (b_l, 0, AH, right),
            (b_r, AH, CA, left),
            (p_l, 0, AH, right),
            (p_r, AH, CA, left),
            (b_own, CA, CW, right),
            (b_own, CA, CW, left),
            (b_own, CA, CW, across),
            (b_l, CA, BH, right),
            (b_r, BH, CW, left),
            (b_l, CA, CW, across),
            (b_r, CA, CW, across),
            (b_o, CA, CW, across),
        )[k]
        ref = xg.at[i, pl.ds(row, 16), lo:hi]
        return send(ref, ref, ag_s.at[i, k], ag_r.at[i, k], to)

    swap_pool.start()
    acc[...] = jnp.zeros_like(acc)

    def gather0(i):
        for k in (0, 1, 2, 9, 10, 11):
            gather(k, i).start()

    def gather1(i):
        gather(0, i).wait_recv()
        gather(3, i).start()
        gather(4, i).start()
        gather(9, i).wait_recv()
        gather(12, i).start()
        gather(14, i).start()
        gather(10, i).wait_recv()
        gather(13, i).start()
        gather(15, i).start()
        gather(1, i).wait_recv()
        gather(5, i).start()
        gather(2, i).wait_recv()
        gather(6, i).start()

    def gather2(i):
        gather(12, i).wait_recv()
        gather(13, i).wait_recv()
        gather(16, i).start()
        gather(3, i).wait_recv()
        gather(7, i).start()
        gather(4, i).wait_recv()
        gather(8, i).start()

    def project(b, n):
        i = b * NN + n
        for k in (5, 6, 7, 8, 11, 14, 15, 16):
            gather(k, i).wait_recv()
        r = pl.ds(pl.multiple_of(n * CW, CW), CW)
        acc[b] += jnp.dot(xg[i], w[r, :], preferred_element_type=F32)

    def gather_step(s, carry):
        @pl.when(s < NC)
        def _():
            gather0(s)

        @pl.when(s < NN)
        def _():
            swap_q(s).start()
            swap_kv(s).start()

        @pl.when(s >= 2)
        def _():
            gather1(s - 2)

        @pl.when(s >= 4)
        def _():
            gather2(s - 4)

        @pl.when(s == 4)
        def _():
            prepare()

        @pl.when(s >= 5)
        def _():
            n = s - 5
            swap_q(n).wait_recv()
            swap_kv(n).wait_recv()
            project(0, n)

        return carry

    def prepare():
        own[0].wait()
        own[1].wait()
        own[2].wait()
        table_in.wait()
        swap_pool.wait_recv()
        swap_wo.start()
        for st in range(2):
            for j in range(MAXP):
                kvc[st, j * PAGE : (j + 1) * PAGE, :] = pool[table_ref[j, st]]
        slot = lax.broadcasted_iota(jnp.int32, (16, 2048), 1)
        page, inside = slot // PAGE, slot % PAGE
        rid = lax.broadcasted_iota(jnp.int32, (16, 1), 0)
        length = jnp.zeros((16, 1), jnp.int32)
        for b in range(16):
            length = jnp.where(rid == b, len_ref[b], length)
        count = jnp.zeros((16, 2048), F32)
        for j in range(MAXP):
            named = jnp.zeros((16, 1), jnp.int32)
            for b in range(16):
                named = jnp.where(rid == b, table_ref[j, 2 + b], named)
            seen = (page == named) & (inside + j * PAGE < length)
            count = count + jnp.where(seen, 1.0, 0.0)
        cnt[...] = count
        for b in range(NB):
            g = row_globals(b, lax.broadcasted_iota(jnp.int32, (128, 1), 0))
            position = jnp.where(g < C, off_ref[0] + g, off_ref[1] + g - C)
            for d in range(16):
                position = jnp.where(g == 2 * C + d, len_ref[d], position)
            angle = position.astype(F32) * freq_ref[...]
            lane = lax.broadcasted_iota(jnp.int32, (128, HD), 1)
            trig[0, b] = jnp.cos(angle)
            trig[1, b] = jnp.where(lane < HD // 2, -jnp.sin(angle), jnp.sin(angle))

    def row_globals(b, lr):
        return ((lr // 16) * 2 + c) * 32 + b * 16 + lr % 16

    def key_globals(row):
        j = row // 256 * 4 + row % 64 // 16
        return (j * 2 + row // 128 % 2) * 32 + row // 64 % 2 * 16 + row % 16

    def rotated(b, col):
        v = acc[b, :, col : col + HD]
        return (v * trig[0, b] + pltpu.roll(v, HD // 2, 1) * trig[1, b]).astype(BF16)

    def swap_new(b, half):
        ref = newkv.at[pl.ds(pl.multiple_of(half * 256 + c * 128 + b * 64, 64), 64)]
        return send(ref, ref, kv_s.at[b, half], kv_r.at[b, half], core_dev)

    def head_rows(b, n):
        lo = B_LO[b]
        return slice(n * (128 - lo), (n + 1) * (128 - lo))

    def place(b):
        k = rotated(b, 512)
        v = acc[b, :, 640:768].astype(BF16)
        for half in range(2):
            rows = pl.ds(pl.multiple_of(half * 256 + c * 128 + b * 64, 64), 64)
            newkv[rows, 0:HD] = k[half * 64 : (half + 1) * 64]
            newkv[rows, HD : 2 * HD] = v[half * 64 : (half + 1) * 64]
        for n in range(4):
            q = rotated(b, n * HD)
            qa[b, n * 64 : (n + 1) * 64, :] = q[0:64]
            qb[b, head_rows(b, n), :] = q[B_LO[b] : 128]
            if b == 1:
                qd[n * 16 : (n + 1) * 16, :] = q[112:128]
            if n == 0:
                swap_new(b, 0).start()
                swap_new(b, 1).start()

    def nt(a, b):
        return lax.dot_general(a, b, (((1,), (1,)), ((), ())), preferred_element_type=F32)

    scale = HD ** (-0.5)

    def queries(b, st):
        return qa[b] if st == 0 else qb[b, 0 : 4 * (128 - B_LO[b]), :]

    def cached(b, st):
        q = queries(b, st)
        n = q.shape[0]
        sc_ref[0:n, :] = nt(q, kvc[st, :, 0:HD])
        slots = lax.broadcasted_iota(jnp.int32, (1, SPAN), 1)
        limit = off_ref[st]

        def some(k, carry):
            rows = pl.ds(pl.multiple_of(k * 32, 32), 32)
            v = jnp.where(slots < limit, sc_ref[rows, :], neg_big)
            m = jnp.max(v, axis=1, keepdims=True)
            e = jnp.exp((v - m) * scale)
            m_ref[b, st, rows, :] = jnp.broadcast_to(m, (32, HD))
            l_ref[b, st, rows, :] = jnp.broadcast_to(jnp.sum(e, axis=1, keepdims=True), (32, HD))
            pc[rows, :] = e.astype(BF16)
            return carry

        lax.fori_loop(0, n // 32, some, 0, unroll=2)
        o_ref[b, st, 0:n, :] = jnp.dot(pc[0:n, :], kvc[st, :, HD : 2 * HD], preferred_element_type=F32)

    def fresh(b, st):
        q = queries(b, st)
        k0, width = (0, 256) if st == 0 else (128, 384)
        n = q.shape[0] // 4
        sf_ref[0 : 4 * n, 0:width] = nt(q, newkv[k0 : k0 + width, 0:HD])
        lo = 0 if st == 0 else B_LO[b]
        kg = key_globals(k0 + lax.broadcasted_iota(jnp.int32, (1, width), 1))
        qg = row_globals(b, lo + lax.broadcasted_iota(jnp.int32, (n, 1), 0))
        seen = (kg <= qg) & (kg < C if st == 0 else kg >= C)
        for head in range(4):
            rows = slice(head * n, (head + 1) * n)
            v = jnp.where(seen, sf_ref[rows, 0:width], neg_big)
            m1 = m_ref[b, st, rows, :]
            m = jnp.maximum(m1, jnp.max(v, axis=1, keepdims=True))
            alpha = jnp.exp((m1 - m) * scale)
            e = jnp.exp((v - m[:, 0:1]) * scale)
            tot = alpha * l_ref[b, st, rows, :] + jnp.sum(e, axis=1, keepdims=True)
            o = jnp.dot(e.astype(BF16), newkv[k0 : k0 + width, HD : 2 * HD], preferred_element_type=F32)
            o = ((alpha * o_ref[b, st, rows, :] + o) / tot).astype(BF16)
            cols = slice(head * HD, (head + 1) * HD)
            if st == 0:
                att[b, 0:64, cols] = o
            elif b == 0:
                att[b, 64:128, cols] = o
            else:
                near = lax.broadcasted_iota(jnp.int32, (16, 1), 0) >= 8 + 8 * (1 - c)
                att[b, 64:128, cols] = o[16:]
                att[b, 48:64, cols] = jnp.where(
                    near, o[0:16].astype(F32), att[b, 48:64, cols].astype(F32)
                ).astype(BF16)

    def decodes():
        for b in range(16):
            sd[:, b * 128 : (b + 1) * 128] = nt(qd[...], pool[b, :, 0:HD])
        self_s = nt(qd[...], newkv[496:512, 0:HD])
        kid = lax.broadcasted_iota(jnp.int32, (64, 16), 1)
        qid = lax.broadcasted_iota(jnp.int32, (64, 16), 0) % 16
        self_s = jnp.where(kid == qid, self_s, neg_big)
        for n in range(4):
            rows = slice(n * 16, (n + 1) * 16)
            own_s = self_s[n * 16 : (n + 1) * 16]
            count = cnt[...]
            v = jnp.where(count > 0.0, sd[rows, :], neg_big)
            m = jnp.maximum(jnp.max(v, axis=1, keepdims=True), jnp.max(own_s, axis=1, keepdims=True))
            e = count * jnp.exp((v - m) * scale)
            e_own = jnp.exp((own_s - m) * scale)
            tot = jnp.sum(e, axis=1, keepdims=True) + jnp.sum(e_own, axis=1, keepdims=True)
            pd[rows, :] = e.astype(BF16)
            o = jnp.dot(e_own.astype(BF16), newkv[496:512, HD : 2 * HD], preferred_element_type=F32)
            for b in range(16):
                o = o + jnp.dot(
                    pd[rows, b * 128 : (b + 1) * 128], pool[b, :, HD : 2 * HD], preferred_element_type=F32
                )
            att[1, 112:128, n * HD : (n + 1) * HD] = (o / tot).astype(BF16)

    lax.fori_loop(0, NC + 1, gather_step, 0)
    place(0)
    gather1(7)
    gather2(5)
    project(1, 0)
    cached(0, 0)
    gather2(6)
    project(1, 1)
    cached(0, 1)
    gather2(7)
    project(1, 2)
    project(1, 3)
    place(1)
    cached(1, 0)
    for b in range(NB):
        swap_new(b, 0).wait_recv()
        swap_new(b, 1).wait_recv()
    fresh(0, 0)
    fresh(0, 1)
    own[3].wait()
    swap_wo.wait_recv()

    def scatter(k, i):
        ss, rr = rs_s.at[i, k], rs_r.at[i, k]
        if k == 0:
            return send(pbuf.at[i, :, xo, :, 0:AH], r_al.at[i], ss, rr, right)
        if k == 1:
            return send(pbuf.at[i, :, xo, :, AH:CA], r_ar.at[i], ss, rr, left)
        if k == 2:
            return send(pbuf.at[i, :, xr, :, 0:CA], r_l.at[i], ss, rr, right)
        if k == 3:
            return send(pbuf.at[i, :, xl, :, 0:CA], r_r.at[i], ss, rr, left)
        if k == 4:
            return send(pbuf.at[i, 1 - h, x, :, 0:CA], r_y.at[i], ss, rr, across)
        if k == 5:
            return send(pbuf.at[i, 1 - h, :, :, CA:CW], s_y.at[i], ss, rr, across)
        if k == 6:
            return send(pbuf.at[i, h, xo, :, CA:BH], s_al.at[i], ss, rr, right)
        if k == 7:
            return send(pbuf.at[i, h, xo, :, BH:CW], s_ar.at[i], ss, rr, left)
        if k == 8:
            return send(pbuf.at[i, h, xr, :, CA:CW], s_l.at[i], ss, rr, right)
        return send(pbuf.at[i, h, xl, :, CA:CW], s_r.at[i], ss, rr, left)

    def f(v):
        return v.astype(F32)

    def scatter0(b, n):
        i = b * NN + n
        for k in range(CW // 256):
            col = pl.multiple_of(n * CW + k * 256, 256)
            prod = jnp.dot(att[b], wo[:, pl.ds(col, 256)], preferred_element_type=F32)
            pbuf[i, :, :, :, k * 256 : (k + 1) * 256] = prod.astype(BF16).reshape(2, 4, 16, 256)
        for k in (0, 1, 5):
            scatter(k, i).start()

    def scatter1(i):
        scatter(0, i).wait_recv()
        pbuf[i, :, xr, :, 0:AH] = (f(pbuf[i, :, xr, :, 0:AH]) + f(r_al[i])).astype(BF16)
        scatter(1, i).wait_recv()
        pbuf[i, :, xl, :, AH:CA] = (f(pbuf[i, :, xl, :, AH:CA]) + f(r_ar[i])).astype(BF16)
        scatter(2, i).start()
        scatter(3, i).start()
        scatter(5, i).wait_recv()
        pbuf[i, h, :, :, CA:CW] = (f(pbuf[i, h, :, :, CA:CW]) + f(s_y[i])).astype(BF16)
        scatter(6, i).start()
        scatter(7, i).start()

    def scatter2(i):
        scatter(2, i).wait_recv()
        scatter(3, i).wait_recv()
        pbuf[i, 1 - h, x, :, 0:CA] = (
            f(pbuf[i, 1 - h, x, :, 0:CA]) + f(r_l[i, 1 - h]) + f(r_r[i, 1 - h])
        ).astype(BF16)
        scatter(4, i).start()
        scatter(6, i).wait_recv()
        pbuf[i, h, xr, :, CA:BH] = (f(pbuf[i, h, xr, :, CA:BH]) + f(s_al[i])).astype(BF16)
        scatter(7, i).wait_recv()
        pbuf[i, h, xl, :, BH:CW] = (f(pbuf[i, h, xl, :, BH:CW]) + f(s_ar[i])).astype(BF16)
        scatter(8, i).start()
        scatter(9, i).start()

    def scatter3(b, n):
        i = b * NN + n
        scatter(4, i).wait_recv()
        rows = pl.ds(pl.multiple_of(b * 16, 16), 16)
        ca = pl.ds(pl.multiple_of(n * CW, 128), CA)
        cb = pl.ds(pl.multiple_of(n * CW + CA, 128), CW - CA)
        out_ref[rows, ca] = (
            f(pbuf[i, h, x, :, 0:CA]) + f(r_l[i, h]) + f(r_r[i, h]) + f(r_y[i])
        ).astype(BF16)
        scatter(8, i).wait_recv()
        scatter(9, i).wait_recv()
        out_ref[rows, cb] = (f(pbuf[i, h, x, :, CA:CW]) + f(s_l[i]) + f(s_r[i])).astype(BF16)

    def first_step(s, carry):
        scatter0(0, s)
        return carry

    lax.fori_loop(0, NN, first_step, 0)
    cached(1, 1)
    scatter1(0)
    fresh(1, 0)
    scatter1(1)
    fresh(1, 1)
    scatter1(2)
    scatter2(0)

    @pl.when(c == 1)
    def _():
        decodes()

    scatter1(3)
    scatter2(1)

    def second_step(s, carry):
        @pl.when(s < NN)
        def _():
            scatter0(1, s)

        @pl.when(s < 2)
        def _():
            scatter2(s + 2)

        @pl.when((s >= 2) & (s < 6))
        def _():
            scatter1(s + 2)

        @pl.when((s >= 4) & (s < 8))
        def _():
            scatter2(s)

        @pl.when(s < 4)
        def _():
            scatter3(0, s)

        @pl.when(s >= 6)
        def _():
            scatter3(1, s - 6)

        return carry

    lax.fori_loop(0, 10, second_step, 0)

    def drain(i, carry):
        for k in range(17):
            gather(k, i).wait_send()
        for k in range(10):
            scatter(k, i).wait_send()
        return carry

    lax.fori_loop(0, NC, drain, 0)
    swap_pool.wait_send()
    swap_wo.wait_send()
    for i in range(NN):
        swap_q(i).wait_send()
        swap_kv(i).wait_send()
    for b in range(NB):
        swap_new(b, 0).wait_send()
        swap_new(b, 1).wait_send()


def shards(x, gain, wq, wkv, wo, pool, table, offsets, lengths):
    half = np.arange(HD) % (HD // 2)
    freq = jnp.asarray((rope_base ** (-2.0 * half / HD)).astype(np.float32))[None]
    vmem = pl.BlockSpec(memory_space=pltpu.VMEM)
    smem = pl.BlockSpec(memory_space=pltpu.SMEM)
    anyw = pl.BlockSpec(memory_space=pl.ANY)
    cb = CW - CA
    dma = pltpu.SemaphoreType.DMA
    return pl.pallas_call(
        kernel,
        name="block",
        out_shape=jax.ShapeDtypeStruct((32, D), BF16),
        in_specs=[anyw, vmem, vmem, anyw, anyw, anyw, anyw, anyw, smem, smem],
        out_specs=vmem,
        scratch_shapes=[
            pltpu.VMEM((32, D), BF16),
            pltpu.SMEM((MAXP, 18), jnp.int32),
            pltpu.VMEM((NC, 128, CW), BF16),
            pltpu.VMEM((D, 768), BF16),
            pltpu.VMEM((512, D), BF16),
            pltpu.VMEM((16, PAGE, 2 * HD), BF16),
            pltpu.VMEM((2, SPAN, 2 * HD), BF16),
            pltpu.VMEM((NB, 128, 768), F32),
            pltpu.VMEM((512, 2 * HD), BF16),
            pltpu.VMEM((NB, 256, HD), BF16),
            pltpu.VMEM((NB, 320, HD), BF16),
            pltpu.VMEM((64, HD), BF16),
            pltpu.VMEM((2, NB, 128, HD), F32),
            pltpu.VMEM((320, SPAN), F32),
            pltpu.VMEM((320, 384), F32),
            pltpu.VMEM((64, 2048), F32),
            pltpu.VMEM((320, SPAN), BF16),
            pltpu.VMEM((64, 2048), BF16),
            pltpu.VMEM((NB, 2, 320, HD), F32),
            pltpu.VMEM((NB, 2, 320, HD), F32),
            pltpu.VMEM((NB, 2, 320, HD), F32),
            pltpu.VMEM((16, 2048), F32),
            pltpu.VMEM((NB, 128, 512), BF16),
            pltpu.VMEM((NC, 2, 4, 16, CW), BF16),
            pltpu.VMEM((NC, 2, 16, AH), BF16),
            pltpu.VMEM((NC, 2, 16, CA - AH), BF16),
            pltpu.VMEM((NC, 2, 16, CA), BF16),
            pltpu.VMEM((NC, 2, 16, CA), BF16),
            pltpu.VMEM((NC, 16, CA), BF16),
            pltpu.VMEM((NC, 4, 16, cb), BF16),
            pltpu.VMEM((NC, 16, BH - CA), BF16),
            pltpu.VMEM((NC, 16, CW - BH), BF16),
            pltpu.VMEM((NC, 16, cb), BF16),
            pltpu.VMEM((NC, 16, cb), BF16),
            dma((2,)),
            dma((4,)),
            dma((2 + 2 * NN,)),
            dma((2 + 2 * NN,)),
            dma((NC, 17)),
            dma((NC, 17)),
            dma((NB, 2)),
            dma((NB, 2)),
            dma((NC, 10)),
            dma((NC, 10)),
        ],
        compiler_params=pltpu.CompilerParams(
            collective_id=0, has_side_effects=True, vmem_limit_bytes=60 * 1024 * 1024
        ),
    )(x, gain[None], freq, wq, wkv, wo, pool, table.T, offsets, lengths)


def solution(mesh):
    placed = (
        P(("req", "tensor"), None),
        P(),
        P(None, "tensor"),
        P(None, "tensor"),
        P("tensor", None),
        P(("req", "tensor"), None, None),
        P("req", None),
        P("req"),
        P("req"),
    )
    return jax.shard_map(
        shards, mesh=mesh, in_specs=placed, out_specs=P(("req", "tensor"), None), check_vma=False
    )
```

```python
import functools

import jax
import jax.numpy as jnp
import numpy as np
from jax import lax
from jax.experimental import pallas as pl
from jax.experimental.pallas import tpu as pltpu
from jax.sharding import PartitionSpec as P

HD = 128
C = 248
PAGE = 128
MAXP = 8
ROWS = 512
D = 8192
CW = 2048
NN = D // CW
NB = 2
NC = NB * NN
CA = 1152
AH = 640
BH = CA + 384
eps_norm = 1e-06
rope_base = 1000000.0
neg_big = -1e30
MESH = pl.DeviceIdType.MESH
F32 = jnp.float32
BF16 = jnp.bfloat16
B_LO = (64, 48)
SPAN = MAXP * PAGE


def kernel(
    x_hbm, gain_hbm, freq_hbm, wq_hbm, wkv_hbm, wo_hbm, pool_hbm, table_hbm, off_hbm, len_hbm,
    out_hbm,
    out_ref, x_ref, gain_ref, freq_ref, table_ref, off_ref, len_ref, xg, w, wo, pool, kvc, acc, newkv, qa, qb, qd, trig, sc_ref, sf_ref, sd, pc, pd,
    m_ref, l_ref, o_ref, cnt, att, pbuf, r_al, r_ar, r_l, r_r, r_y, s_y, s_al, s_ar, s_l, s_r,
    in_sem, out_sem, own_sem, ws_sem, wr_sem, ag_s, ag_r, kv_s, kv_r, rs_s, rs_r,
):
    req = lax.axis_index("req")
    me = lax.axis_index("tensor")
    h, x, c = me // 8, (me // 2) % 4, me % 2

    def dev(hh, xx, cc):
        return (req, hh * 8 + xx * 2 + cc)

    xr, xl, xo = lax.rem(x + 1, 4), lax.rem(x + 3, 4), lax.rem(x + 2, 4)
    core_dev, right, left, across = dev(h, x, 1 - c), dev(h, xr, c), dev(h, xl, c), dev(1 - h, x, c)

    def send(src, dst, ssem, rsem, to):
        return pltpu.make_async_remote_copy(
            src_ref=src, dst_ref=dst, send_sem=ssem, recv_sem=rsem, device_id=to, device_id_type=MESH
        )

    barrier = pltpu.get_barrier_semaphore()
    for to in (core_dev, right, left, across):
        pl.semaphore_signal(barrier, inc=1, device_id=to, device_id_type=MESH)

    inputs = [
        pltpu.make_async_copy(src, dst, in_sem.at[k])
        for k, (src, dst) in enumerate(
            (
                (x_hbm, x_ref),
                (gain_hbm, gain_ref),
                (freq_hbm, freq_ref),
                (table_hbm, table_ref),
                (off_hbm, off_ref),
                (len_hbm, len_ref),
            )
        )
    ]
    for copy in inputs:
        copy.start()

    qcol = pl.multiple_of(c * 256, 256)
    kcol = pl.multiple_of(512 + c * 128, 128)
    orow = pl.multiple_of(c * 256, 256)
    prow = c * 8
    own = [
        pltpu.make_async_copy(pool_hbm, pool.at[pl.ds(prow, 8)], own_sem.at[0]),
        pltpu.make_async_copy(wq_hbm, w.at[:, pl.ds(qcol, 256)], own_sem.at[1]),
        pltpu.make_async_copy(wkv_hbm, w.at[:, pl.ds(kcol, 128)], own_sem.at[2]),
        pltpu.make_async_copy(wo_hbm, wo.at[pl.ds(orow, 256)], own_sem.at[3]),
    ]
    mine = pl.multiple_of((h * 4 + x) * 16, 16)
    total = jnp.zeros((32, 1), F32)
    inputs[0].wait()
    inputs[1].wait()
    for copy in own:
        copy.start()
    for i in range(NN):
        v = x_ref[:, i * CW : (i + 1) * CW].astype(F32)
        total = total + jnp.sum(v * v, axis=1, keepdims=True)
    inv = lax.rsqrt(total * (1.0 / D) + eps_norm)
    for i in range(NN):
        v = x_ref[:, i * CW : (i + 1) * CW].astype(F32)
        v = (v * inv * gain_ref[:, i * CW : (i + 1) * CW]).astype(BF16)
        for b in range(NB):
            xg[b * NN + i, pl.ds(mine, 16), :] = v[b * 16 : (b + 1) * 16]

    pl.semaphore_wait(barrier, 4)

    swap_pool = send(pool_hbm, pool.at[pl.ds(prow, 8)], ws_sem.at[0], wr_sem.at[0], core_dev)
    swap_wo = send(wo_hbm, wo.at[pl.ds(orow, 256)], ws_sem.at[1], wr_sem.at[1], core_dev)

    def swap_q(i):
        r = pl.ds(pl.multiple_of(i * CW, CW), CW)
        return send(wq_hbm.at[r], w.at[r, pl.ds(qcol, 256)], ws_sem.at[2 + i], wr_sem.at[2 + i], core_dev)

    def swap_kv(i):
        r = pl.ds(pl.multiple_of(i * CW, CW), CW)
        return send(
            wkv_hbm.at[r], w.at[r, pl.ds(kcol, 128)], ws_sem.at[2 + NN + i], wr_sem.at[2 + NN + i], core_dev
        )

    def block(hh, xx):
        return pl.multiple_of((hh * 4 + xx) * 16, 16)

    b_own, b_par = block(h, x), block(1 - h, x)
    b_l, b_r, b_o = block(h, xl), block(h, xr), block(h, xo)
    p_l, p_r = block(1 - h, xl), block(1 - h, xr)

    def gather(k, i):
        row, lo, hi, to = (
            (b_own, 0, CA, across),
            (b_own, 0, CA, right),
            (b_own, 0, CA, left),
            (b_par, 0, CA, right),
            (b_par, 0, CA, left),
            (b_l, 0, AH, right),
            (b_r, AH, CA, left),
            (p_l, 0, AH, right),
            (p_r, AH, CA, left),
            (b_own, CA, CW, right),
            (b_own, CA, CW, left),
            (b_own, CA, CW, across),
            (b_l, CA, BH, right),
            (b_r, BH, CW, left),
            (b_l, CA, CW, across),
            (b_r, CA, CW, across),
            (b_o, CA, CW, across),
        )[k]
        ref = xg.at[i, pl.ds(row, 16), lo:hi]
        return send(ref, ref, ag_s.at[i, k], ag_r.at[i, k], to)

    swap_pool.start()
    acc[...] = jnp.zeros_like(acc)

    def gather0(i):
        for k in (0, 1, 2, 9, 10, 11):
            gather(k, i).start()

    def gather1(i):
        gather(0, i).wait_recv()
        gather(3, i).start()
        gather(4, i).start()
        gather(9, i).wait_recv()
        gather(12, i).start()
        gather(14, i).start()
        gather(10, i).wait_recv()
        gather(13, i).start()
        gather(15, i).start()
        gather(1, i).wait_recv()
        gather(5, i).start()
        gather(2, i).wait_recv()
        gather(6, i).start()

    def gather2(i):
        gather(12, i).wait_recv()
        gather(13, i).wait_recv()
        gather(16, i).start()
        gather(3, i).wait_recv()
        gather(7, i).start()
        gather(4, i).wait_recv()
        gather(8, i).start()

    def arrived(i):
        for k in (5, 6, 7, 8, 11, 14, 15, 16):
            gather(k, i).wait_recv()

    def project(b, n, lo=0, hi=768):
        r = pl.ds(pl.multiple_of(n * CW, CW), CW)
        acc[b, :, lo:hi] += jnp.dot(xg[b * NN + n], w[r, lo:hi], preferred_element_type=F32)

    def gather_step(s, carry):
        @pl.when(s < NC)
        def _():
            gather0(s)

        @pl.when(s < NN)
        def _():
            swap_q(s).start()
            swap_kv(s).start()

        @pl.when(s >= 2)
        def _():
            gather1(s - 2)

        @pl.when(s >= 4)
        def _():
            gather2(s - 4)

        @pl.when(s == 4)
        def _():
            prepare()

        @pl.when(s >= 5)
        def _():
            n = s - 5
            swap_q(n).wait_recv()
            swap_kv(n).wait_recv()
            arrived(n)
            project(0, n)

        return carry

    def prepare():
        own[0].wait()
        own[1].wait()
        own[2].wait()
        for copy in inputs[2:]:
            copy.wait()
        swap_pool.wait_recv()
        swap_wo.start()
        for st in range(2):
            for j in range(MAXP):
                kvc[st, j * PAGE : (j + 1) * PAGE, :] = pool[table_ref[j, st]]
        slot = lax.broadcasted_iota(jnp.int32, (16, 2048), 1)
        page, inside = slot // PAGE, slot % PAGE
        rid = lax.broadcasted_iota(jnp.int32, (16, 1), 0)
        length = jnp.zeros((16, 1), jnp.int32)
        for b in range(16):
            length = jnp.where(rid == b, len_ref[b], length)
        count = jnp.zeros((16, 2048), F32)
        for j in range(MAXP):
            named = jnp.zeros((16, 1), jnp.int32)
            for b in range(16):
                named = jnp.where(rid == b, table_ref[j, 2 + b], named)
            seen = (page == named) & (inside + j * PAGE < length)
            count = count + jnp.where(seen, 1.0, 0.0)
        cnt[...] = count
        for b in range(NB):
            g = row_globals(b, lax.broadcasted_iota(jnp.int32, (128, 1), 0))
            position = jnp.where(g < C, off_ref[0] + g, off_ref[1] + g - C)
            for d in range(16):
                position = jnp.where(g == 2 * C + d, len_ref[d], position)
            angle = position.astype(F32) * freq_ref[...]
            lane = lax.broadcasted_iota(jnp.int32, (128, HD), 1)
            trig[0, b] = jnp.cos(angle)
            trig[1, b] = jnp.where(lane < HD // 2, -jnp.sin(angle), jnp.sin(angle))

    def row_globals(b, lr):
        return ((lr // 16) * 2 + c) * 32 + b * 16 + lr % 16

    def key_globals(row):
        j = row // 256 * 4 + row % 64 // 16
        return (j * 2 + row // 128 % 2) * 32 + row // 64 % 2 * 16 + row % 16

    def rotated(b, col):
        v = acc[b, :, col : col + HD]
        return (v * trig[0, b] + pltpu.roll(v, HD // 2, 1) * trig[1, b]).astype(BF16)

    def swap_new(b, half):
        ref = newkv.at[pl.ds(pl.multiple_of(half * 256 + c * 128 + b * 64, 64), 64)]
        return send(ref, ref, kv_s.at[b, half], kv_r.at[b, half], core_dev)

    def head_rows(b, n):
        lo = B_LO[b]
        return slice(n * (128 - lo), (n + 1) * (128 - lo))

    def place_new(b):
        k = rotated(b, 512)
        v = acc[b, :, 640:768].astype(BF16)
        for half in range(2):
            rows = pl.ds(pl.multiple_of(half * 256 + c * 128 + b * 64, 64), 64)
            newkv[rows, 0:HD] = k[half * 64 : (half + 1) * 64]
            newkv[rows, HD : 2 * HD] = v[half * 64 : (half + 1) * 64]

    def place_queries(b):
        for n in range(4):
            q = rotated(b, n * HD)
            qa[b, n * 64 : (n + 1) * 64, :] = q[0:64]
            qb[b, head_rows(b, n), :] = q[B_LO[b] : 128]
            if b == 1:
                qd[n * 16 : (n + 1) * 16, :] = q[112:128]

    def exchange(b):
        swap_new(b, 0).start()
        swap_new(b, 1).start()

    def nt(a, b):
        return lax.dot_general(a, b, (((1,), (1,)), ((), ())), preferred_element_type=F32)

    scale = HD ** (-0.5)

    def queries(b, st):
        return qa[b] if st == 0 else qb[b, 0 : 4 * (128 - B_LO[b]), :]

    def cached(b, st):
        q = queries(b, st)
        n = q.shape[0]
        sc_ref[0:n, :] = nt(q, kvc[st, :, 0:HD])
        slots = lax.broadcasted_iota(jnp.int32, (1, SPAN), 1)
        limit = off_ref[st]

        def some(k, carry):
            rows = pl.ds(pl.multiple_of(k * 32, 32), 32)
            v = jnp.where(slots < limit, sc_ref[rows, :], neg_big)
            m = jnp.max(v, axis=1, keepdims=True)
            e = jnp.exp((v - m) * scale)
            m_ref[b, st, rows, :] = jnp.broadcast_to(m, (32, HD))
            l_ref[b, st, rows, :] = jnp.broadcast_to(jnp.sum(e, axis=1, keepdims=True), (32, HD))
            pc[rows, :] = e.astype(BF16)
            return carry

        lax.fori_loop(0, n // 32, some, 0, unroll=2)
        o_ref[b, st, 0:n, :] = jnp.dot(pc[0:n, :], kvc[st, :, HD : 2 * HD], preferred_element_type=F32)

    def fresh(b, st):
        q = queries(b, st)
        k0, width = (0, 256) if st == 0 else (128, 384)
        n = q.shape[0] // 4
        sf_ref[0 : 4 * n, 0:width] = nt(q, newkv[k0 : k0 + width, 0:HD])
        lo = 0 if st == 0 else B_LO[b]
        kg = key_globals(k0 + lax.broadcasted_iota(jnp.int32, (1, width), 1))
        qg = row_globals(b, lo + lax.broadcasted_iota(jnp.int32, (n, 1), 0))
        seen = (kg <= qg) & (kg < C if st == 0 else kg >= C)
        for head in range(4):
            rows = slice(head * n, (head + 1) * n)
            v = jnp.where(seen, sf_ref[rows, 0:width], neg_big)
            m1 = m_ref[b, st, rows, :]
            m = jnp.maximum(m1, jnp.max(v, axis=1, keepdims=True))
            alpha = jnp.exp((m1 - m) * scale)
            e = jnp.exp((v - m[:, 0:1]) * scale)
            tot = alpha * l_ref[b, st, rows, :] + jnp.sum(e, axis=1, keepdims=True)
            o = jnp.dot(e.astype(BF16), newkv[k0 : k0 + width, HD : 2 * HD], preferred_element_type=F32)
            o = ((alpha * o_ref[b, st, rows, :] + o) / tot).astype(BF16)
            cols = slice(head * HD, (head + 1) * HD)
            if st == 0:
                att[b, 0:64, cols] = o
            elif b == 0:
                att[b, 64:128, cols] = o
            else:
                near = lax.broadcasted_iota(jnp.int32, (16, 1), 0) >= 8 + 8 * (1 - c)
                att[b, 64:128, cols] = o[16:]
                att[b, 48:64, cols] = jnp.where(
                    near, o[0:16].astype(F32), att[b, 48:64, cols].astype(F32)
                ).astype(BF16)

    def decodes():
        for b in range(16):
            sd[:, b * 128 : (b + 1) * 128] = nt(qd[...], pool[b, :, 0:HD])
        self_s = nt(qd[...], newkv[496:512, 0:HD])
        kid = lax.broadcasted_iota(jnp.int32, (64, 16), 1)
        qid = lax.broadcasted_iota(jnp.int32, (64, 16), 0) % 16
        self_s = jnp.where(kid == qid, self_s, neg_big)
        for n in range(4):
            rows = slice(n * 16, (n + 1) * 16)
            own_s = self_s[n * 16 : (n + 1) * 16]
            count = cnt[...]
            v = jnp.where(count > 0.0, sd[rows, :], neg_big)
            m = jnp.maximum(jnp.max(v, axis=1, keepdims=True), jnp.max(own_s, axis=1, keepdims=True))
            e = count * jnp.exp((v - m) * scale)
            e_own = jnp.exp((own_s - m) * scale)
            tot = jnp.sum(e, axis=1, keepdims=True) + jnp.sum(e_own, axis=1, keepdims=True)
            pd[rows, :] = e.astype(BF16)
            o = jnp.dot(e_own.astype(BF16), newkv[496:512, HD : 2 * HD], preferred_element_type=F32)
            for b in range(16):
                o = o + jnp.dot(
                    pd[rows, b * 128 : (b + 1) * 128], pool[b, :, HD : 2 * HD], preferred_element_type=F32
                )
            att[1, 112:128, n * HD : (n + 1) * HD] = (o / tot).astype(BF16)

    lax.fori_loop(0, NC + 1, gather_step, 0)
    gather1(7)
    gather2(5)
    place_new(0)
    place_queries(0)
    exchange(0)
    cached(0, 0)
    gather2(6)
    cached(0, 1)
    gather2(7)
    arrived(4)
    project(1, 0)
    arrived(5)
    project(1, 1)
    arrived(6)
    project(1, 2)
    arrived(7)
    project(1, 3, 512, 768)
    place_new(1)
    project(1, 3, 0, 256)
    exchange(1)
    project(1, 3, 256, 512)
    place_queries(1)
    for b in range(NB):
        swap_new(b, 0).wait_recv()
        swap_new(b, 1).wait_recv()
    fresh(0, 0)
    fresh(0, 1)
    own[3].wait()
    swap_wo.wait_recv()

    def scatter(k, i):
        ss, rr = rs_s.at[i, k], rs_r.at[i, k]
        if k == 0:
            return send(pbuf.at[i, :, xo, :, 0:AH], r_al.at[i], ss, rr, right)
        if k == 1:
            return send(pbuf.at[i, :, xo, :, AH:CA], r_ar.at[i], ss, rr, left)
        if k == 2:
            return send(pbuf.at[i, :, xr, :, 0:CA], r_l.at[i], ss, rr, right)
        if k == 3:
            return send(pbuf.at[i, :, xl, :, 0:CA], r_r.at[i], ss, rr, left)
        if k == 4:
            return send(pbuf.at[i, 1 - h, x, :, 0:CA], r_y.at[i], ss, rr, across)
        if k == 5:
            return send(pbuf.at[i, 1 - h, :, :, CA:CW], s_y.at[i], ss, rr, across)
        if k == 6:
            return send(pbuf.at[i, h, xo, :, CA:BH], s_al.at[i], ss, rr, right)
        if k == 7:
            return send(pbuf.at[i, h, xo, :, BH:CW], s_ar.at[i], ss, rr, left)
        if k == 8:
            return send(pbuf.at[i, h, xr, :, CA:CW], s_l.at[i], ss, rr, right)
        return send(pbuf.at[i, h, xl, :, CA:CW], s_r.at[i], ss, rr, left)

    def f(v):
        return v.astype(F32)

    def scatter0(b, n):
        i = b * NN + n
        for k in range(CW // 256):
            col = pl.multiple_of(n * CW + k * 256, 256)
            prod = jnp.dot(att[b], wo[:, pl.ds(col, 256)], preferred_element_type=F32)
            pbuf[i, :, :, :, k * 256 : (k + 1) * 256] = prod.astype(BF16).reshape(2, 4, 16, 256)
        for k in (0, 1, 5):
            scatter(k, i).start()

    def scatter1(i):
        scatter(0, i).wait_recv()
        pbuf[i, :, xr, :, 0:AH] = (f(pbuf[i, :, xr, :, 0:AH]) + f(r_al[i])).astype(BF16)
        scatter(1, i).wait_recv()
        pbuf[i, :, xl, :, AH:CA] = (f(pbuf[i, :, xl, :, AH:CA]) + f(r_ar[i])).astype(BF16)
        scatter(2, i).start()
        scatter(3, i).start()
        scatter(5, i).wait_recv()
        pbuf[i, h, :, :, CA:CW] = (f(pbuf[i, h, :, :, CA:CW]) + f(s_y[i])).astype(BF16)
        scatter(6, i).start()
        scatter(7, i).start()

    def scatter2(i):
        scatter(2, i).wait_recv()
        scatter(3, i).wait_recv()
        pbuf[i, 1 - h, x, :, 0:CA] = (
            f(pbuf[i, 1 - h, x, :, 0:CA]) + f(r_l[i, 1 - h]) + f(r_r[i, 1 - h])
        ).astype(BF16)
        scatter(4, i).start()
        scatter(6, i).wait_recv()
        pbuf[i, h, xr, :, CA:BH] = (f(pbuf[i, h, xr, :, CA:BH]) + f(s_al[i])).astype(BF16)
        scatter(7, i).wait_recv()
        pbuf[i, h, xl, :, BH:CW] = (f(pbuf[i, h, xl, :, BH:CW]) + f(s_ar[i])).astype(BF16)
        scatter(8, i).start()
        scatter(9, i).start()

    def scatter3(b, n):
        i = b * NN + n
        scatter(4, i).wait_recv()
        rows = pl.ds(pl.multiple_of(b * 16, 16), 16)
        ca = pl.ds(pl.multiple_of(n * CW, 128), CA)
        cb = pl.ds(pl.multiple_of(n * CW + CA, 128), CW - CA)
        out_ref[rows, ca] = (
            f(pbuf[i, h, x, :, 0:CA]) + f(r_l[i, h]) + f(r_r[i, h]) + f(r_y[i])
        ).astype(BF16)
        scatter(8, i).wait_recv()
        scatter(9, i).wait_recv()
        out_ref[rows, cb] = (f(pbuf[i, h, x, :, CA:CW]) + f(s_l[i]) + f(s_r[i])).astype(BF16)

    def written(b, n):
        rows = pl.ds(pl.multiple_of(b * 16, 16), 16)
        cols = pl.ds(pl.multiple_of(n * CW, 128), CW)
        return pltpu.make_async_copy(out_ref.at[rows, cols], out_hbm.at[rows, cols], out_sem.at[b * NN + n])

    def first_step(s, carry):
        scatter0(0, s)
        return carry

    lax.fori_loop(0, NN, first_step, 0)
    cached(1, 0)
    scatter1(0)
    cached(1, 1)
    scatter1(1)
    fresh(1, 0)
    fresh(1, 1)
    scatter1(2)
    scatter2(0)

    @pl.when(c == 1)
    def _():
        decodes()

    scatter1(3)
    scatter2(1)

    def second_step(s, carry):
        @pl.when(s < NN)
        def _():
            scatter0(1, s)

        @pl.when(s < 2)
        def _():
            scatter2(s + 2)

        @pl.when((s >= 2) & (s < 6))
        def _():
            scatter1(s + 2)

        @pl.when((s >= 4) & (s < 8))
        def _():
            scatter2(s)

        @pl.when(s < 4)
        def _():
            scatter3(0, s)
            written(0, s).start()

        @pl.when(s >= 6)
        def _():
            scatter3(1, s - 6)
            written(1, s - 6).start()

        return carry

    lax.fori_loop(0, 10, second_step, 0)

    def drain(i, carry):
        for k in range(17):
            gather(k, i).wait_send()
        for k in range(10):
            scatter(k, i).wait_send()
        return carry

    lax.fori_loop(0, NC, drain, 0)
    swap_pool.wait_send()
    swap_wo.wait_send()
    for i in range(NN):
        for b in range(NB):
            written(b, i).wait()
        swap_q(i).wait_send()
        swap_kv(i).wait_send()
    for b in range(NB):
        swap_new(b, 0).wait_send()
        swap_new(b, 1).wait_send()


def shards(x, gain, wq, wkv, wo, pool, table, offsets, lengths):
    half = np.arange(HD) % (HD // 2)
    freq = jnp.asarray((rope_base ** (-2.0 * half / HD)).astype(np.float32))[None]
    anyw = pl.BlockSpec(memory_space=pl.ANY)
    cb = CW - CA
    dma = pltpu.SemaphoreType.DMA
    return pl.pallas_call(
        kernel,
        name="block",
        out_shape=jax.ShapeDtypeStruct((32, D), BF16),
        in_specs=[anyw] * 10,
        out_specs=anyw,
        scratch_shapes=[
            pltpu.VMEM((32, D), BF16),
            pltpu.VMEM((32, D), BF16),
            pltpu.VMEM((1, D), F32),
            pltpu.VMEM((1, HD), F32),
            pltpu.SMEM((MAXP, 18), jnp.int32),
            pltpu.SMEM((2,), jnp.int32),
            pltpu.SMEM((16,), jnp.int32),
            pltpu.VMEM((NC, 128, CW), BF16),
            pltpu.VMEM((D, 768), BF16),
            pltpu.VMEM((512, D), BF16),
            pltpu.VMEM((16, PAGE, 2 * HD), BF16),
            pltpu.VMEM((2, SPAN, 2 * HD), BF16),
            pltpu.VMEM((NB, 128, 768), F32),
            pltpu.VMEM((512, 2 * HD), BF16),
            pltpu.VMEM((NB, 256, HD), BF16),
            pltpu.VMEM((NB, 320, HD), BF16),
            pltpu.VMEM((64, HD), BF16),
            pltpu.VMEM((2, NB, 128, HD), F32),
            pltpu.VMEM((320, SPAN), F32),
            pltpu.VMEM((320, 384), F32),
            pltpu.VMEM((64, 2048), F32),
            pltpu.VMEM((320, SPAN), BF16),
            pltpu.VMEM((64, 2048), BF16),
            pltpu.VMEM((NB, 2, 320, HD), F32),
            pltpu.VMEM((NB, 2, 320, HD), F32),
            pltpu.VMEM((NB, 2, 320, HD), F32),
            pltpu.VMEM((16, 2048), F32),
            pltpu.VMEM((NB, 128, 512), BF16),
            pltpu.VMEM((NC, 2, 4, 16, CW), BF16),
            pltpu.VMEM((NC, 2, 16, AH), BF16),
            pltpu.VMEM((NC, 2, 16, CA - AH), BF16),
            pltpu.VMEM((NC, 2, 16, CA), BF16),
            pltpu.VMEM((NC, 2, 16, CA), BF16),
            pltpu.VMEM((NC, 16, CA), BF16),
            pltpu.VMEM((NC, 4, 16, cb), BF16),
            pltpu.VMEM((NC, 16, BH - CA), BF16),
            pltpu.VMEM((NC, 16, CW - BH), BF16),
            pltpu.VMEM((NC, 16, cb), BF16),
            pltpu.VMEM((NC, 16, cb), BF16),
            dma((6,)),
            dma((NC,)),
            dma((4,)),
            dma((2 + 2 * NN,)),
            dma((2 + 2 * NN,)),
            dma((NC, 17)),
            dma((NC, 17)),
            dma((NB, 2)),
            dma((NB, 2)),
            dma((NC, 10)),
            dma((NC, 10)),
        ],
        compiler_params=pltpu.CompilerParams(
            collective_id=0, has_side_effects=True, vmem_limit_bytes=60 * 1024 * 1024
        ),
    )(x, gain[None], freq, wq, wkv, wo, pool, table.T, offsets, lengths)


def solution(mesh):
    placed = (
        P(("req", "tensor"), None),
        P(),
        P(None, "tensor"),
        P(None, "tensor"),
        P("tensor", None),
        P(("req", "tensor"), None, None),
        P("req", None),
        P("req"),
        P("req"),
    )
    return jax.shard_map(
        shards, mesh=mesh, in_specs=placed, out_specs=P(("req", "tensor"), None), check_vma=False
    )
```

```python
import functools

import jax
import jax.numpy as jnp
import numpy as np
from jax import lax
from jax.experimental import pallas as pl
from jax.experimental.pallas import tpu as pltpu
from jax.sharding import PartitionSpec as P

HD = 128
C = 248
PAGE = 128
MAXP = 8
ROWS = 512
D = 8192
CW = 2048
NN = D // CW
NB = 2
NC = NB * NN
CA = 1152
AH = 640
BH = CA + 384
eps_norm = 1e-06
rope_base = 1000000.0
neg_big = -1e30
MESH = pl.DeviceIdType.MESH
F32 = jnp.float32
BF16 = jnp.bfloat16
B_LO = (64, 48)
SPAN = MAXP * PAGE


def kernel(
    x_hbm, gain_hbm, freq_hbm, wq_hbm, wkv_hbm, wo_hbm, pool_hbm, table_hbm, off_hbm, len_hbm,
    out_hbm,
    out_ref, x_ref, gain_ref, freq_ref, table_ref, off_ref, len_ref, xg, w, wo, pool, kvc, acc, newkv, qa, qb, qd, trig, sc_ref, sf_ref, sd, pc, pd,
    m_ref, l_ref, o_ref, cnt, att, pbuf, r_al, r_ar, r_l, r_r, r_y, s_y, s_al, s_ar, s_l, s_r,
    in_sem, out_sem, own_sem, ws_sem, wr_sem, ag_s, ag_r, kv_s, kv_r, rs_s, rs_r,
):
    req = lax.axis_index("req")
    me = lax.axis_index("tensor")
    h, x, c = me // 8, (me // 2) % 4, me % 2

    def dev(hh, xx, cc):
        return (req, hh * 8 + xx * 2 + cc)

    xr, xl, xo = lax.rem(x + 1, 4), lax.rem(x + 3, 4), lax.rem(x + 2, 4)
    core_dev, right, left, across = dev(h, x, 1 - c), dev(h, xr, c), dev(h, xl, c), dev(1 - h, x, c)

    def send(src, dst, ssem, rsem, to):
        return pltpu.make_async_remote_copy(
            src_ref=src, dst_ref=dst, send_sem=ssem, recv_sem=rsem, device_id=to, device_id_type=MESH
        )

    barrier = pltpu.get_barrier_semaphore()
    for to in (core_dev, right, left, across):
        pl.semaphore_signal(barrier, inc=1, device_id=to, device_id_type=MESH)

    inputs = [
        pltpu.make_async_copy(src, dst, in_sem.at[k])
        for k, (src, dst) in enumerate(
            (
                (x_hbm, x_ref),
                (gain_hbm, gain_ref),
                (freq_hbm, freq_ref),
                (table_hbm, table_ref),
                (off_hbm, off_ref),
                (len_hbm, len_ref),
            )
        )
    ]
    for copy in inputs:
        copy.start()

    qcol = pl.multiple_of(c * 256, 256)
    kcol = pl.multiple_of(512 + c * 128, 128)
    orow = pl.multiple_of(c * 256, 256)
    prow = c * 8
    own = [
        pltpu.make_async_copy(pool_hbm, pool.at[pl.ds(prow, 8)], own_sem.at[0]),
        pltpu.make_async_copy(wq_hbm, w.at[:, pl.ds(qcol, 256)], own_sem.at[1]),
        pltpu.make_async_copy(wkv_hbm, w.at[:, pl.ds(kcol, 128)], own_sem.at[2]),
        pltpu.make_async_copy(wo_hbm, wo.at[pl.ds(orow, 256)], own_sem.at[3]),
    ]
    mine = pl.multiple_of((h * 4 + x) * 16, 16)
    total = jnp.zeros((32, 1), F32)
    inputs[0].wait()
    inputs[1].wait()
    for copy in own:
        copy.start()
    for i in range(NN):
        v = x_ref[:, i * CW : (i + 1) * CW].astype(F32)
        total = total + jnp.sum(v * v, axis=1, keepdims=True)
    inv = lax.rsqrt(total * (1.0 / D) + eps_norm)
    for i in range(NN):
        v = x_ref[:, i * CW : (i + 1) * CW].astype(F32)
        v = (v * inv * gain_ref[:, i * CW : (i + 1) * CW]).astype(BF16)
        for b in range(NB):
            xg[b * NN + i, pl.ds(mine, 16), :] = v[b * 16 : (b + 1) * 16]

    pl.semaphore_wait(barrier, 4)

    swap_pool = send(pool_hbm, pool.at[pl.ds(prow, 8)], ws_sem.at[0], wr_sem.at[0], core_dev)
    swap_wo = send(wo_hbm, wo.at[pl.ds(orow, 256)], ws_sem.at[1], wr_sem.at[1], core_dev)

    def swap_q(i):
        r = pl.ds(pl.multiple_of(i * CW, CW), CW)
        return send(wq_hbm.at[r], w.at[r, pl.ds(qcol, 256)], ws_sem.at[2 + i], wr_sem.at[2 + i], core_dev)

    def swap_kv(i):
        r = pl.ds(pl.multiple_of(i * CW, CW), CW)
        return send(
            wkv_hbm.at[r], w.at[r, pl.ds(kcol, 128)], ws_sem.at[2 + NN + i], wr_sem.at[2 + NN + i], core_dev
        )

    def block(hh, xx):
        return pl.multiple_of((hh * 4 + xx) * 16, 16)

    b_own, b_par = block(h, x), block(1 - h, x)
    b_l, b_r, b_o = block(h, xl), block(h, xr), block(h, xo)
    p_l, p_r = block(1 - h, xl), block(1 - h, xr)

    def gather(k, i):
        row, lo, hi, to = (
            (b_own, 0, CA, across),
            (b_own, 0, CA, right),
            (b_own, 0, CA, left),
            (b_par, 0, CA, right),
            (b_par, 0, CA, left),
            (b_l, 0, AH, right),
            (b_r, AH, CA, left),
            (p_l, 0, AH, right),
            (p_r, AH, CA, left),
            (b_own, CA, CW, right),
            (b_own, CA, CW, left),
            (b_own, CA, CW, across),
            (b_l, CA, BH, right),
            (b_r, BH, CW, left),
            (b_l, CA, CW, across),
            (b_r, CA, CW, across),
            (b_o, CA, CW, across),
        )[k]
        ref = xg.at[i, pl.ds(row, 16), lo:hi]
        return send(ref, ref, ag_s.at[i, k], ag_r.at[i, k], to)

    swap_pool.start()
    acc[...] = jnp.zeros_like(acc)

    def gather0(i):
        for k in (0, 1, 2, 9, 10, 11):
            gather(k, i).start()

    def gather1(i):
        gather(0, i).wait_recv()
        gather(3, i).start()
        gather(4, i).start()
        gather(9, i).wait_recv()
        gather(12, i).start()
        gather(14, i).start()
        gather(10, i).wait_recv()
        gather(13, i).start()
        gather(15, i).start()
        gather(1, i).wait_recv()
        gather(5, i).start()
        gather(2, i).wait_recv()
        gather(6, i).start()

    def gather2(i):
        gather(12, i).wait_recv()
        gather(13, i).wait_recv()
        gather(16, i).start()
        gather(3, i).wait_recv()
        gather(7, i).start()
        gather(4, i).wait_recv()
        gather(8, i).start()

    def arrived(i):
        for k in (5, 6, 7, 8, 11, 14, 15, 16):
            gather(k, i).wait_recv()

    def project(b, n, lo=0, hi=768):
        r = pl.ds(pl.multiple_of(n * CW, CW), CW)
        acc[b, :, lo:hi] += jnp.dot(xg[b * NN + n], w[r, lo:hi], preferred_element_type=F32)

    def gather_step(s, carry):
        @pl.when(s < NC)
        def _():
            gather0(s)

        @pl.when(s < NN)
        def _():
            swap_q(s).start()
            swap_kv(s).start()

        @pl.when(s >= 2)
        def _():
            gather1(s - 2)

        @pl.when(s >= 4)
        def _():
            gather2(s - 4)

        @pl.when(s == 4)
        def _():
            prepare()

        @pl.when(s >= 5)
        def _():
            n = s - 5
            swap_q(n).wait_recv()
            swap_kv(n).wait_recv()
            arrived(n)
            project(0, n)

        return carry

    def prepare():
        own[0].wait()
        own[1].wait()
        own[2].wait()
        for copy in inputs[2:]:
            copy.wait()
        swap_pool.wait_recv()
        swap_wo.start()
        for st in range(2):
            for j in range(MAXP):
                kvc[st, j * PAGE : (j + 1) * PAGE, :] = pool[table_ref[j, st]]
        slot = lax.broadcasted_iota(jnp.int32, (16, 2048), 1)
        page, inside = slot // PAGE, slot % PAGE
        rid = lax.broadcasted_iota(jnp.int32, (16, 1), 0)
        length = jnp.zeros((16, 1), jnp.int32)
        for b in range(16):
            length = jnp.where(rid == b, len_ref[b], length)
        count = jnp.zeros((16, 2048), F32)
        for j in range(MAXP):
            named = jnp.zeros((16, 1), jnp.int32)
            for b in range(16):
                named = jnp.where(rid == b, table_ref[j, 2 + b], named)
            seen = (page == named) & (inside + j * PAGE < length)
            count = count + jnp.where(seen, 1.0, 0.0)
        cnt[...] = count
        for b in range(NB):
            g = row_globals(b, lax.broadcasted_iota(jnp.int32, (128, 1), 0))
            position = jnp.where(g < C, off_ref[0] + g, off_ref[1] + g - C)
            for d in range(16):
                position = jnp.where(g == 2 * C + d, len_ref[d], position)
            angle = position.astype(F32) * freq_ref[...]
            lane = lax.broadcasted_iota(jnp.int32, (128, HD), 1)
            trig[0, b] = jnp.cos(angle)
            trig[1, b] = jnp.where(lane < HD // 2, -jnp.sin(angle), jnp.sin(angle))

    def row_globals(b, lr):
        return ((lr // 16) * 2 + c) * 32 + b * 16 + lr % 16

    def key_globals(row):
        j = row // 256 * 4 + row % 64 // 16
        return (j * 2 + row // 128 % 2) * 32 + row // 64 % 2 * 16 + row % 16

    def rotated(b, col):
        v = acc[b, :, col : col + HD]
        return (v * trig[0, b] + pltpu.roll(v, HD // 2, 1) * trig[1, b]).astype(BF16)

    def swap_new(b, half):
        ref = newkv.at[pl.ds(pl.multiple_of(half * 256 + c * 128 + b * 64, 64), 64)]
        return send(ref, ref, kv_s.at[b, half], kv_r.at[b, half], core_dev)

    def head_rows(b, n):
        lo = B_LO[b]
        return slice(n * (128 - lo), (n + 1) * (128 - lo))

    def place_new(b):
        k = rotated(b, 512)
        v = acc[b, :, 640:768].astype(BF16)
        for half in range(2):
            rows = pl.ds(pl.multiple_of(half * 256 + c * 128 + b * 64, 64), 64)
            newkv[rows, 0:HD] = k[half * 64 : (half + 1) * 64]
            newkv[rows, HD : 2 * HD] = v[half * 64 : (half + 1) * 64]

    def place_queries(b):
        for n in range(4):
            q = rotated(b, n * HD)
            qa[b, n * 64 : (n + 1) * 64, :] = q[0:64]
            qb[b, head_rows(b, n), :] = q[B_LO[b] : 128]
            if b == 1:
                qd[n * 16 : (n + 1) * 16, :] = q[112:128]

    def exchange(b):
        swap_new(b, 0).start()
        swap_new(b, 1).start()

    def nt(a, b):
        return lax.dot_general(a, b, (((1,), (1,)), ((), ())), preferred_element_type=F32)

    scale = HD ** (-0.5)

    def queries(b, st):
        return qa[b] if st == 0 else qb[b, 0 : 4 * (128 - B_LO[b]), :]

    def cached(b, st):
        q = queries(b, st)
        n = q.shape[0]
        sc_ref[0:n, :] = nt(q, kvc[st, :, 0:HD])
        slots = lax.broadcasted_iota(jnp.int32, (1, SPAN), 1)
        limit = off_ref[st]

        def some(k, carry):
            rows = pl.ds(pl.multiple_of(k * 32, 32), 32)
            v = jnp.where(slots < limit, sc_ref[rows, :], neg_big)
            m = jnp.max(v, axis=1, keepdims=True)
            e = jnp.exp((v - m) * scale)
            m_ref[b, st, rows, :] = jnp.broadcast_to(m, (32, HD))
            l_ref[b, st, rows, :] = jnp.broadcast_to(jnp.sum(e, axis=1, keepdims=True), (32, HD))
            pc[rows, :] = e.astype(BF16)
            return carry

        lax.fori_loop(0, n // 32, some, 0, unroll=2)
        o_ref[b, st, 0:n, :] = jnp.dot(pc[0:n, :], kvc[st, :, HD : 2 * HD], preferred_element_type=F32)

    def fresh(b, st):
        q = queries(b, st)
        k0, width = (0, 256) if st == 0 else (128, 384)
        n = q.shape[0] // 4
        sf_ref[0 : 4 * n, 0:width] = nt(q, newkv[k0 : k0 + width, 0:HD])
        lo = 0 if st == 0 else B_LO[b]
        kg = key_globals(k0 + lax.broadcasted_iota(jnp.int32, (1, width), 1))
        qg = row_globals(b, lo + lax.broadcasted_iota(jnp.int32, (n, 1), 0))
        seen = (kg <= qg) & (kg < C if st == 0 else kg >= C)
        for head in range(4):
            rows = slice(head * n, (head + 1) * n)
            v = jnp.where(seen, sf_ref[rows, 0:width], neg_big)
            m1 = m_ref[b, st, rows, :]
            m = jnp.maximum(m1, jnp.max(v, axis=1, keepdims=True))
            alpha = jnp.exp((m1 - m) * scale)
            e = jnp.exp((v - m[:, 0:1]) * scale)
            tot = alpha * l_ref[b, st, rows, :] + jnp.sum(e, axis=1, keepdims=True)
            o = jnp.dot(e.astype(BF16), newkv[k0 : k0 + width, HD : 2 * HD], preferred_element_type=F32)
            o = ((alpha * o_ref[b, st, rows, :] + o) / tot).astype(BF16)
            cols = slice(head * HD, (head + 1) * HD)
            if st == 0:
                att[b, 0:64, cols] = o
            elif b == 0:
                att[b, 64:128, cols] = o
            else:
                near = lax.broadcasted_iota(jnp.int32, (16, 1), 0) >= 8 + 8 * (1 - c)
                att[b, 64:128, cols] = o[16:]
                att[b, 48:64, cols] = jnp.where(
                    near, o[0:16].astype(F32), att[b, 48:64, cols].astype(F32)
                ).astype(BF16)

    def decodes():
        for b in range(16):
            sd[:, b * 128 : (b + 1) * 128] = nt(qd[...], pool[b, :, 0:HD])
        self_s = nt(qd[...], newkv[496:512, 0:HD])
        kid = lax.broadcasted_iota(jnp.int32, (64, 16), 1)
        qid = lax.broadcasted_iota(jnp.int32, (64, 16), 0) % 16
        self_s = jnp.where(kid == qid, self_s, neg_big)
        for n in range(4):
            rows = slice(n * 16, (n + 1) * 16)
            own_s = self_s[n * 16 : (n + 1) * 16]
            count = cnt[...]
            v = jnp.where(count > 0.0, sd[rows, :], neg_big)
            m = jnp.maximum(jnp.max(v, axis=1, keepdims=True), jnp.max(own_s, axis=1, keepdims=True))
            e = count * jnp.exp((v - m) * scale)
            e_own = jnp.exp((own_s - m) * scale)
            tot = jnp.sum(e, axis=1, keepdims=True) + jnp.sum(e_own, axis=1, keepdims=True)
            pd[rows, :] = e.astype(BF16)
            o = jnp.dot(e_own.astype(BF16), newkv[496:512, HD : 2 * HD], preferred_element_type=F32)
            for b in range(16):
                o = o + jnp.dot(
                    pd[rows, b * 128 : (b + 1) * 128], pool[b, :, HD : 2 * HD], preferred_element_type=F32
                )
            att[1, 112:128, n * HD : (n + 1) * HD] = (o / tot).astype(BF16)

    lax.fori_loop(0, NC + 1, gather_step, 0)
    gather1(7)
    gather2(5)
    place_new(0)
    place_queries(0)
    exchange(0)
    cached(0, 0)
    gather2(6)
    cached(0, 1)
    gather2(7)
    arrived(4)
    project(1, 0)
    arrived(5)
    project(1, 1)
    arrived(6)
    project(1, 2)
    arrived(7)
    project(1, 3, 512, 768)
    place_new(1)
    project(1, 3, 0, 256)
    exchange(1)
    project(1, 3, 256, 512)
    place_queries(1)
    for b in range(NB):
        swap_new(b, 0).wait_recv()
        swap_new(b, 1).wait_recv()
    fresh(0, 0)
    fresh(0, 1)
    own[3].wait()
    swap_wo.wait_recv()

    def scatter(k, i):
        ss, rr = rs_s.at[i, k], rs_r.at[i, k]
        if k == 0:
            return send(pbuf.at[i, :, xo, :, 0:AH], r_al.at[i], ss, rr, right)
        if k == 1:
            return send(pbuf.at[i, :, xo, :, AH:CA], r_ar.at[i], ss, rr, left)
        if k == 2:
            return send(pbuf.at[i, :, xr, :, 0:CA], r_l.at[i], ss, rr, right)
        if k == 3:
            return send(pbuf.at[i, :, xl, :, 0:CA], r_r.at[i], ss, rr, left)
        if k == 4:
            return send(pbuf.at[i, 1 - h, x, :, 0:CA], r_y.at[i], ss, rr, across)
        if k == 5:
            return send(pbuf.at[i, 1 - h, :, :, CA:CW], s_y.at[i], ss, rr, across)
        if k == 6:
            return send(pbuf.at[i, h, xo, :, CA:BH], s_al.at[i], ss, rr, right)
        if k == 7:
            return send(pbuf.at[i, h, xo, :, BH:CW], s_ar.at[i], ss, rr, left)
        if k == 8:
            return send(pbuf.at[i, h, xr, :, CA:CW], s_l.at[i], ss, rr, right)
        return send(pbuf.at[i, h, xl, :, CA:CW], s_r.at[i], ss, rr, left)

    def f(v):
        return v.astype(F32)

    def scatter0(b, n):
        i = b * NN + n
        for k in range(CW // 256):
            col = pl.multiple_of(n * CW + k * 256, 256)
            prod = jnp.dot(att[b], wo[:, pl.ds(col, 256)], preferred_element_type=F32)
            pbuf[i, :, :, :, k * 256 : (k + 1) * 256] = prod.astype(BF16).reshape(2, 4, 16, 256)
        for k in (0, 1, 5):
            scatter(k, i).start()

    def scatter1(i):
        scatter(0, i).wait_recv()
        pbuf[i, :, xr, :, 0:AH] = (f(pbuf[i, :, xr, :, 0:AH]) + f(r_al[i])).astype(BF16)
        scatter(1, i).wait_recv()
        pbuf[i, :, xl, :, AH:CA] = (f(pbuf[i, :, xl, :, AH:CA]) + f(r_ar[i])).astype(BF16)
        scatter(2, i).start()
        scatter(3, i).start()
        scatter(5, i).wait_recv()
        pbuf[i, h, :, :, CA:CW] = (f(pbuf[i, h, :, :, CA:CW]) + f(s_y[i])).astype(BF16)
        scatter(6, i).start()
        scatter(7, i).start()

    def scatter2(i):
        scatter(2, i).wait_recv()
        scatter(3, i).wait_recv()
        pbuf[i, 1 - h, x, :, 0:CA] = (
            f(pbuf[i, 1 - h, x, :, 0:CA]) + f(r_l[i, 1 - h]) + f(r_r[i, 1 - h])
        ).astype(BF16)
        scatter(4, i).start()
        scatter(6, i).wait_recv()
        pbuf[i, h, xr, :, CA:BH] = (f(pbuf[i, h, xr, :, CA:BH]) + f(s_al[i])).astype(BF16)
        scatter(7, i).wait_recv()
        pbuf[i, h, xl, :, BH:CW] = (f(pbuf[i, h, xl, :, BH:CW]) + f(s_ar[i])).astype(BF16)
        scatter(8, i).start()
        scatter(9, i).start()

    def scatter3(b, n):
        i = b * NN + n
        scatter(4, i).wait_recv()
        rows = pl.ds(pl.multiple_of(b * 16, 16), 16)
        ca = pl.ds(pl.multiple_of(n * CW, 128), CA)
        cb = pl.ds(pl.multiple_of(n * CW + CA, 128), CW - CA)
        out_ref[rows, ca] = (
            f(pbuf[i, h, x, :, 0:CA]) + f(r_l[i, h]) + f(r_r[i, h]) + f(r_y[i])
        ).astype(BF16)
        scatter(8, i).wait_recv()
        scatter(9, i).wait_recv()
        out_ref[rows, cb] = (f(pbuf[i, h, x, :, CA:CW]) + f(s_l[i]) + f(s_r[i])).astype(BF16)

    def written(b, n):
        rows = pl.ds(pl.multiple_of(b * 16, 16), 16)
        cols = pl.ds(pl.multiple_of(n * CW, 128), CW)
        return pltpu.make_async_copy(out_ref.at[rows, cols], out_hbm.at[rows, cols], out_sem.at[b * NN + n])

    def first_step(s, carry):
        scatter0(0, s)
        return carry

    lax.fori_loop(0, NN, first_step, 0)
    cached(1, 0)
    cached(1, 1)
    fresh(1, 0)
    fresh(1, 1)

    @pl.when(c == 1)
    def _():
        decodes()

    scatter1(0)
    scatter1(1)

    def second_step(s, carry):
        @pl.when(s < NC)
        def _():
            scatter0(1, s - NN)

        @pl.when(s < NC + 2)
        def _():
            scatter1(s - 2)

        @pl.when(s < NC + 4)
        def _():
            scatter2(s - 4)

        @pl.when(s >= 6)
        def _():
            i = s - 6
            scatter3(i // NN, i % NN)
            written(i // NN, i % NN).start()

        return carry

    lax.fori_loop(NN, NC + 6, second_step, 0)

    def drain(i, carry):
        for k in range(17):
            gather(k, i).wait_send()
        for k in range(10):
            scatter(k, i).wait_send()
        return carry

    lax.fori_loop(0, NC, drain, 0)
    swap_pool.wait_send()
    swap_wo.wait_send()
    for i in range(NN):
        for b in range(NB):
            written(b, i).wait()
        swap_q(i).wait_send()
        swap_kv(i).wait_send()
    for b in range(NB):
        swap_new(b, 0).wait_send()
        swap_new(b, 1).wait_send()


def shards(x, gain, wq, wkv, wo, pool, table, offsets, lengths):
    half = np.arange(HD) % (HD // 2)
    freq = jnp.asarray((rope_base ** (-2.0 * half / HD)).astype(np.float32))[None]
    anyw = pl.BlockSpec(memory_space=pl.ANY)
    cb = CW - CA
    dma = pltpu.SemaphoreType.DMA
    return pl.pallas_call(
        kernel,
        name="block",
        out_shape=jax.ShapeDtypeStruct((32, D), BF16),
        in_specs=[anyw] * 10,
        out_specs=anyw,
        scratch_shapes=[
            pltpu.VMEM((32, D), BF16),
            pltpu.VMEM((32, D), BF16),
            pltpu.VMEM((1, D), F32),
            pltpu.VMEM((1, HD), F32),
            pltpu.SMEM((MAXP, 18), jnp.int32),
            pltpu.SMEM((2,), jnp.int32),
            pltpu.SMEM((16,), jnp.int32),
            pltpu.VMEM((NC, 128, CW), BF16),
            pltpu.VMEM((D, 768), BF16),
            pltpu.VMEM((512, D), BF16),
            pltpu.VMEM((16, PAGE, 2 * HD), BF16),
            pltpu.VMEM((2, SPAN, 2 * HD), BF16),
            pltpu.VMEM((NB, 128, 768), F32),
            pltpu.VMEM((512, 2 * HD), BF16),
            pltpu.VMEM((NB, 256, HD), BF16),
            pltpu.VMEM((NB, 320, HD), BF16),
            pltpu.VMEM((64, HD), BF16),
            pltpu.VMEM((2, NB, 128, HD), F32),
            pltpu.VMEM((320, SPAN), F32),
            pltpu.VMEM((320, 384), F32),
            pltpu.VMEM((64, 2048), F32),
            pltpu.VMEM((320, SPAN), BF16),
            pltpu.VMEM((64, 2048), BF16),
            pltpu.VMEM((NB, 2, 320, HD), F32),
            pltpu.VMEM((NB, 2, 320, HD), F32),
            pltpu.VMEM((NB, 2, 320, HD), F32),
            pltpu.VMEM((16, 2048), F32),
            pltpu.VMEM((NB, 128, 512), BF16),
            pltpu.VMEM((NC, 2, 4, 16, CW), BF16),
            pltpu.VMEM((NC, 2, 16, AH), BF16),
            pltpu.VMEM((NC, 2, 16, CA - AH), BF16),
            pltpu.VMEM((NC, 2, 16, CA), BF16),
            pltpu.VMEM((NC, 2, 16, CA), BF16),
            pltpu.VMEM((NC, 16, CA), BF16),
            pltpu.VMEM((NC, 4, 16, cb), BF16),
            pltpu.VMEM((NC, 16, BH - CA), BF16),
            pltpu.VMEM((NC, 16, CW - BH), BF16),
            pltpu.VMEM((NC, 16, cb), BF16),
            pltpu.VMEM((NC, 16, cb), BF16),
            dma((6,)),
            dma((NC,)),
            dma((4,)),
            dma((2 + 2 * NN,)),
            dma((2 + 2 * NN,)),
            dma((NC, 17)),
            dma((NC, 17)),
            dma((NB, 2)),
            dma((NB, 2)),
            dma((NC, 10)),
            dma((NC, 10)),
        ],
        compiler_params=pltpu.CompilerParams(
            collective_id=0, has_side_effects=True, vmem_limit_bytes=60 * 1024 * 1024
        ),
    )(x, gain[None], freq, wq, wkv, wo, pool, table.T, offsets, lengths)


def solution(mesh):
    placed = (
        P(("req", "tensor"), None),
        P(),
        P(None, "tensor"),
        P(None, "tensor"),
        P("tensor", None),
        P(("req", "tensor"), None, None),
        P("req", None),
        P("req"),
        P("req"),
    )
    return jax.shard_map(
        shards, mesh=mesh, in_specs=placed, out_specs=P(("req", "tensor"), None), check_vma=False
    )
```

```python
import functools

import jax
import jax.numpy as jnp
import numpy as np
from jax import lax
from jax.experimental import pallas as pl
from jax.experimental.pallas import tpu as pltpu
from jax.sharding import PartitionSpec as P

HD = 128
C = 248
PAGE = 128
MAXP = 8
ROWS = 512
D = 8192
CW = 2048
NN = D // CW
NB = 2
NC = NB * NN
CA = 1152
AH = 640
BH = CA + 384
eps_norm = 1e-06
rope_base = 1000000.0
neg_big = -1e30
MESH = pl.DeviceIdType.MESH
F32 = jnp.float32
BF16 = jnp.bfloat16
B_LO = (64, 48)
SPAN = MAXP * PAGE


def kernel(
    x_hbm, gain_hbm, freq_hbm, wq_hbm, wkv_hbm, wo_hbm, pool_hbm, table_hbm, off_hbm, len_hbm,
    out_hbm,
    out_ref, x_ref, gain_ref, freq_ref, table_ref, off_ref, len_ref, xg, w, wo, pool, kvc, acc, newkv, qa, qb, qd, trig, sc_ref, sf_ref, sd, pc, pd,
    m_ref, l_ref, o_ref, cnt, att, pbuf, r_al, r_ar, r_l, r_r, r_y, s_y, s_al, s_ar, s_l, s_r,
    in_sem, out_sem, own_sem, ws_sem, wr_sem, ag_s, ag_r, kv_s, kv_r, rs_s, rs_r,
):
    req = lax.axis_index("req")
    me = lax.axis_index("tensor")
    h, x, c = me // 8, (me // 2) % 4, me % 2

    def dev(hh, xx, cc):
        return (req, hh * 8 + xx * 2 + cc)

    xr, xl, xo = lax.rem(x + 1, 4), lax.rem(x + 3, 4), lax.rem(x + 2, 4)
    core_dev, right, left, across = dev(h, x, 1 - c), dev(h, xr, c), dev(h, xl, c), dev(1 - h, x, c)

    def send(src, dst, ssem, rsem, to):
        return pltpu.make_async_remote_copy(
            src_ref=src, dst_ref=dst, send_sem=ssem, recv_sem=rsem, device_id=to, device_id_type=MESH
        )

    barrier = pltpu.get_barrier_semaphore()
    for to in (core_dev, right, left, across):
        pl.semaphore_signal(barrier, inc=1, device_id=to, device_id_type=MESH)

    inputs = [
        pltpu.make_async_copy(src, dst, in_sem.at[k])
        for k, (src, dst) in enumerate(
            (
                (x_hbm, x_ref),
                (gain_hbm, gain_ref),
                (freq_hbm, freq_ref),
                (table_hbm, table_ref),
                (off_hbm, off_ref),
                (len_hbm, len_ref),
            )
        )
    ]
    for copy in inputs:
        copy.start()

    qcol = pl.multiple_of(c * 256, 256)
    kcol = pl.multiple_of(512 + c * 128, 128)
    orow = pl.multiple_of(c * 256, 256)
    prow = c * 8
    own = [
        pltpu.make_async_copy(pool_hbm, pool.at[pl.ds(prow, 8)], own_sem.at[0]),
        pltpu.make_async_copy(wq_hbm, w.at[:, pl.ds(qcol, 256)], own_sem.at[1]),
        pltpu.make_async_copy(wkv_hbm, w.at[:, pl.ds(kcol, 128)], own_sem.at[2]),
        pltpu.make_async_copy(wo_hbm, wo.at[pl.ds(orow, 256)], own_sem.at[3]),
    ]
    mine = pl.multiple_of((h * 4 + x) * 16, 16)
    total = jnp.zeros((32, 1), F32)
    inputs[0].wait()
    inputs[1].wait()
    for copy in own:
        copy.start()
    for i in range(NN):
        v = x_ref[:, i * CW : (i + 1) * CW].astype(F32)
        total = total + jnp.sum(v * v, axis=1, keepdims=True)
    inv = lax.rsqrt(total * (1.0 / D) + eps_norm)
    for i in range(NN):
        v = x_ref[:, i * CW : (i + 1) * CW].astype(F32)
        v = (v * inv * gain_ref[:, i * CW : (i + 1) * CW]).astype(BF16)
        for b in range(NB):
            xg[b * NN + i, pl.ds(mine, 16), :] = v[b * 16 : (b + 1) * 16]

    pl.semaphore_wait(barrier, 4)

    swap_pool = send(pool_hbm, pool.at[pl.ds(prow, 8)], ws_sem.at[0], wr_sem.at[0], core_dev)
    swap_wo = send(wo_hbm, wo.at[pl.ds(orow, 256)], ws_sem.at[1], wr_sem.at[1], core_dev)

    def swap_q(i):
        r = pl.ds(pl.multiple_of(i * CW, CW), CW)
        return send(wq_hbm.at[r], w.at[r, pl.ds(qcol, 256)], ws_sem.at[2 + i], wr_sem.at[2 + i], core_dev)

    def swap_kv(i):
        r = pl.ds(pl.multiple_of(i * CW, CW), CW)
        return send(
            wkv_hbm.at[r], w.at[r, pl.ds(kcol, 128)], ws_sem.at[2 + NN + i], wr_sem.at[2 + NN + i], core_dev
        )

    def block(hh, xx):
        return pl.multiple_of((hh * 4 + xx) * 16, 16)

    b_own, b_par = block(h, x), block(1 - h, x)
    b_l, b_r, b_o = block(h, xl), block(h, xr), block(h, xo)
    p_l, p_r = block(1 - h, xl), block(1 - h, xr)

    def gather(k, i):
        row, lo, hi, to = (
            (b_own, 0, CA, across),
            (b_own, 0, CA, right),
            (b_own, 0, CA, left),
            (b_par, 0, CA, right),
            (b_par, 0, CA, left),
            (b_l, 0, AH, right),
            (b_r, AH, CA, left),
            (p_l, 0, AH, right),
            (p_r, AH, CA, left),
            (b_own, CA, CW, right),
            (b_own, CA, CW, left),
            (b_own, CA, CW, across),
            (b_l, CA, BH, right),
            (b_r, BH, CW, left),
            (b_l, CA, CW, across),
            (b_r, CA, CW, across),
            (b_o, CA, CW, across),
        )[k]
        ref = xg.at[i, pl.ds(row, 16), lo:hi]
        return send(ref, ref, ag_s.at[i, k], ag_r.at[i, k], to)

    swap_pool.start()
    acc[...] = jnp.zeros_like(acc)

    def gather0(i):
        for k in (0, 1, 2, 9, 10, 11):
            gather(k, i).start()

    def gather1(i):
        gather(0, i).wait_recv()
        gather(3, i).start()
        gather(4, i).start()
        gather(9, i).wait_recv()
        gather(12, i).start()
        gather(14, i).start()
        gather(10, i).wait_recv()
        gather(13, i).start()
        gather(15, i).start()
        gather(1, i).wait_recv()
        gather(5, i).start()
        gather(2, i).wait_recv()
        gather(6, i).start()

    def gather2(i):
        gather(12, i).wait_recv()
        gather(13, i).wait_recv()
        gather(16, i).start()
        gather(3, i).wait_recv()
        gather(7, i).start()
        gather(4, i).wait_recv()
        gather(8, i).start()

    def arrived(i):
        for k in (5, 6, 7, 8, 11, 14, 15, 16):
            gather(k, i).wait_recv()

    def project(b, n, lo=0, hi=768):
        r = pl.ds(pl.multiple_of(n * CW, CW), CW)
        acc[b, :, lo:hi] += jnp.dot(xg[b * NN + n], w[r, lo:hi], preferred_element_type=F32)

    def gather_step(s, carry):
        @pl.when(s < NC)
        def _():
            gather0(s)

        @pl.when(s < NN)
        def _():
            swap_q(s).start()
            swap_kv(s).start()

        @pl.when(s >= 2)
        def _():
            gather1(s - 2)

        @pl.when(s >= 4)
        def _():
            gather2(s - 4)

        @pl.when(s == 4)
        def _():
            prepare()

        @pl.when(s >= 5)
        def _():
            n = s - 5
            swap_q(n).wait_recv()
            swap_kv(n).wait_recv()
            arrived(n)
            project(0, n)

        return carry

    def prepare():
        own[0].wait()
        own[1].wait()
        own[2].wait()
        for copy in inputs[2:]:
            copy.wait()
        swap_pool.wait_recv()
        swap_wo.start()
        for st in range(2):
            for j in range(MAXP):
                kvc[st, j * PAGE : (j + 1) * PAGE, :] = pool[table_ref[j, st]]
        slot = lax.broadcasted_iota(jnp.int32, (16, 2048), 1)
        page, inside = slot // PAGE, slot % PAGE
        rid = lax.broadcasted_iota(jnp.int32, (16, 1), 0)
        length = jnp.zeros((16, 1), jnp.int32)
        for b in range(16):
            length = jnp.where(rid == b, len_ref[b], length)
        count = jnp.zeros((16, 2048), F32)
        for j in range(MAXP):
            named = jnp.zeros((16, 1), jnp.int32)
            for b in range(16):
                named = jnp.where(rid == b, table_ref[j, 2 + b], named)
            seen = (page == named) & (inside + j * PAGE < length)
            count = count + jnp.where(seen, 1.0, 0.0)
        cnt[...] = count
        for b in range(NB):
            g = row_globals(b, lax.broadcasted_iota(jnp.int32, (128, 1), 0))
            position = jnp.where(g < C, off_ref[0] + g, off_ref[1] + g - C)
            for d in range(16):
                position = jnp.where(g == 2 * C + d, len_ref[d], position)
            angle = position.astype(F32) * freq_ref[...]
            lane = lax.broadcasted_iota(jnp.int32, (128, HD), 1)
            trig[0, b] = jnp.cos(angle)
            trig[1, b] = jnp.where(lane < HD // 2, -jnp.sin(angle), jnp.sin(angle))

    def row_globals(b, lr):
        return ((lr // 16) * 2 + c) * 32 + b * 16 + lr % 16

    def key_globals(row):
        j = row // 256 * 4 + row % 64 // 16
        return (j * 2 + row // 128 % 2) * 32 + row // 64 % 2 * 16 + row % 16

    def rotated(b, col):
        v = acc[b, :, col : col + HD]
        return (v * trig[0, b] + pltpu.roll(v, HD // 2, 1) * trig[1, b]).astype(BF16)

    def swap_new(b, half):
        ref = newkv.at[pl.ds(pl.multiple_of(half * 256 + c * 128 + b * 64, 64), 64)]
        return send(ref, ref, kv_s.at[b, half], kv_r.at[b, half], core_dev)

    def head_rows(b, n):
        lo = B_LO[b]
        return slice(n * (128 - lo), (n + 1) * (128 - lo))

    def place_new(b):
        k = rotated(b, 512)
        v = acc[b, :, 640:768].astype(BF16)
        for half in range(2):
            rows = pl.ds(pl.multiple_of(half * 256 + c * 128 + b * 64, 64), 64)
            newkv[rows, 0:HD] = k[half * 64 : (half + 1) * 64]
            newkv[rows, HD : 2 * HD] = v[half * 64 : (half + 1) * 64]

    def place_queries(b):
        for n in range(4):
            q = rotated(b, n * HD)
            qa[b, n * 64 : (n + 1) * 64, :] = q[0:64]
            qb[b, head_rows(b, n), :] = q[B_LO[b] : 128]
            if b == 1:
                qd[n * 16 : (n + 1) * 16, :] = q[112:128]

    def exchange(b):
        swap_new(b, 0).start()
        swap_new(b, 1).start()

    def nt(a, b):
        return lax.dot_general(a, b, (((1,), (1,)), ((), ())), preferred_element_type=F32)

    scale = HD ** (-0.5)

    def queries(b, st):
        return qa[b] if st == 0 else qb[b, 0 : 4 * (128 - B_LO[b]), :]

    def cached(b, st):
        q = queries(b, st)
        n = q.shape[0]
        sc_ref[0:n, :] = nt(q, kvc[st, :, 0:HD])
        slots = lax.broadcasted_iota(jnp.int32, (1, SPAN), 1)
        limit = off_ref[st]

        def some(k, carry):
            rows = pl.ds(pl.multiple_of(k * 32, 32), 32)
            v = jnp.where(slots < limit, sc_ref[rows, :], neg_big)
            m = jnp.max(v, axis=1, keepdims=True)
            e = jnp.exp((v - m) * scale)
            m_ref[b, st, rows, :] = jnp.broadcast_to(m, (32, HD))
            l_ref[b, st, rows, :] = jnp.broadcast_to(jnp.sum(e, axis=1, keepdims=True), (32, HD))
            pc[rows, :] = e.astype(BF16)
            return carry

        lax.fori_loop(0, n // 32, some, 0, unroll=True)
        o_ref[b, st, 0:n, :] = jnp.dot(pc[0:n, :], kvc[st, :, HD : 2 * HD], preferred_element_type=F32)

    def fresh(b, st):
        q = queries(b, st)
        k0, width = (0, 256) if st == 0 else (128, 384)
        n = q.shape[0] // 4
        sf_ref[0 : 4 * n, 0:width] = nt(q, newkv[k0 : k0 + width, 0:HD])
        lo = 0 if st == 0 else B_LO[b]
        kg = key_globals(k0 + lax.broadcasted_iota(jnp.int32, (1, width), 1))
        qg = row_globals(b, lo + lax.broadcasted_iota(jnp.int32, (n, 1), 0))
        seen = (kg <= qg) & (kg < C if st == 0 else kg >= C)
        for head in range(4):
            rows = slice(head * n, (head + 1) * n)
            v = jnp.where(seen, sf_ref[rows, 0:width], neg_big)
            m1 = m_ref[b, st, rows, :]
            m = jnp.maximum(m1, jnp.max(v, axis=1, keepdims=True))
            alpha = jnp.exp((m1 - m) * scale)
            e = jnp.exp((v - m[:, 0:1]) * scale)
            tot = alpha * l_ref[b, st, rows, :] + jnp.sum(e, axis=1, keepdims=True)
            o = jnp.dot(e.astype(BF16), newkv[k0 : k0 + width, HD : 2 * HD], preferred_element_type=F32)
            o = ((alpha * o_ref[b, st, rows, :] + o) / tot).astype(BF16)
            cols = slice(head * HD, (head + 1) * HD)
            if st == 0:
                att[b, 0:64, cols] = o
            elif b == 0:
                att[b, 64:128, cols] = o
            else:
                near = lax.broadcasted_iota(jnp.int32, (16, 1), 0) >= 8 + 8 * (1 - c)
                att[b, 64:128, cols] = o[16:]
                att[b, 48:64, cols] = jnp.where(
                    near, o[0:16].astype(F32), att[b, 48:64, cols].astype(F32)
                ).astype(BF16)

    def decodes():
        for b in range(16):
            sd[:, b * 128 : (b + 1) * 128] = nt(qd[...], pool[b, :, 0:HD])
        self_s = nt(qd[...], newkv[496:512, 0:HD])
        kid = lax.broadcasted_iota(jnp.int32, (64, 16), 1)
        qid = lax.broadcasted_iota(jnp.int32, (64, 16), 0) % 16
        self_s = jnp.where(kid == qid, self_s, neg_big)
        for n in range(4):
            rows = slice(n * 16, (n + 1) * 16)
            own_s = self_s[n * 16 : (n + 1) * 16]
            count = cnt[...]
            v = jnp.where(count > 0.0, sd[rows, :], neg_big)
            m = jnp.maximum(jnp.max(v, axis=1, keepdims=True), jnp.max(own_s, axis=1, keepdims=True))
            e = count * jnp.exp((v - m) * scale)
            e_own = jnp.exp((own_s - m) * scale)
            tot = jnp.sum(e, axis=1, keepdims=True) + jnp.sum(e_own, axis=1, keepdims=True)
            pd[rows, :] = e.astype(BF16)
            o = jnp.dot(e_own.astype(BF16), newkv[496:512, HD : 2 * HD], preferred_element_type=F32)
            for b in range(16):
                o = o + jnp.dot(
                    pd[rows, b * 128 : (b + 1) * 128], pool[b, :, HD : 2 * HD], preferred_element_type=F32
                )
            att[1, 112:128, n * HD : (n + 1) * HD] = (o / tot).astype(BF16)

    lax.fori_loop(0, NC + 1, gather_step, 0)
    gather1(7)
    gather2(5)
    place_new(0)
    place_queries(0)
    exchange(0)
    cached(0, 0)
    gather2(6)
    cached(0, 1)
    gather2(7)
    arrived(4)
    project(1, 0)
    arrived(5)
    project(1, 1)
    arrived(6)
    project(1, 2)
    arrived(7)
    project(1, 3, 512, 768)
    place_new(1)
    project(1, 3, 0, 256)
    exchange(1)
    project(1, 3, 256, 512)
    place_queries(1)
    for b in range(NB):
        swap_new(b, 0).wait_recv()
        swap_new(b, 1).wait_recv()
    fresh(0, 0)
    fresh(0, 1)
    own[3].wait()
    swap_wo.wait_recv()

    def scatter(k, i):
        ss, rr = rs_s.at[i, k], rs_r.at[i, k]
        if k == 0:
            return send(pbuf.at[i, :, xo, :, 0:AH], r_al.at[i], ss, rr, right)
        if k == 1:
            return send(pbuf.at[i, :, xo, :, AH:CA], r_ar.at[i], ss, rr, left)
        if k == 2:
            return send(pbuf.at[i, :, xr, :, 0:CA], r_l.at[i], ss, rr, right)
        if k == 3:
            return send(pbuf.at[i, :, xl, :, 0:CA], r_r.at[i], ss, rr, left)
        if k == 4:
            return send(pbuf.at[i, 1 - h, x, :, 0:CA], r_y.at[i], ss, rr, across)
        if k == 5:
            return send(pbuf.at[i, 1 - h, :, :, CA:CW], s_y.at[i], ss, rr, across)
        if k == 6:
            return send(pbuf.at[i, h, xo, :, CA:BH], s_al.at[i], ss, rr, right)
        if k == 7:
            return send(pbuf.at[i, h, xo, :, BH:CW], s_ar.at[i], ss, rr, left)
        if k == 8:
            return send(pbuf.at[i, h, xr, :, CA:CW], s_l.at[i], ss, rr, right)
        return send(pbuf.at[i, h, xl, :, CA:CW], s_r.at[i], ss, rr, left)

    def f(v):
        return v.astype(F32)

    def scatter0(b, n):
        i = b * NN + n
        for k in range(CW // 256):
            col = pl.multiple_of(n * CW + k * 256, 256)
            prod = jnp.dot(att[b], wo[:, pl.ds(col, 256)], preferred_element_type=F32)
            pbuf[i, :, :, :, k * 256 : (k + 1) * 256] = prod.astype(BF16).reshape(2, 4, 16, 256)
        for k in (0, 1, 5):
            scatter(k, i).start()

    def scatter1(i):
        scatter(0, i).wait_recv()
        pbuf[i, :, xr, :, 0:AH] = (f(pbuf[i, :, xr, :, 0:AH]) + f(r_al[i])).astype(BF16)
        scatter(1, i).wait_recv()
        pbuf[i, :, xl, :, AH:CA] = (f(pbuf[i, :, xl, :, AH:CA]) + f(r_ar[i])).astype(BF16)
        scatter(2, i).start()
        scatter(3, i).start()
        scatter(5, i).wait_recv()
        pbuf[i, h, :, :, CA:CW] = (f(pbuf[i, h, :, :, CA:CW]) + f(s_y[i])).astype(BF16)
        scatter(6, i).start()
        scatter(7, i).start()

    def scatter2(i):
        scatter(2, i).wait_recv()
        scatter(3, i).wait_recv()
        pbuf[i, 1 - h, x, :, 0:CA] = (
            f(pbuf[i, 1 - h, x, :, 0:CA]) + f(r_l[i, 1 - h]) + f(r_r[i, 1 - h])
        ).astype(BF16)
        scatter(4, i).start()
        scatter(6, i).wait_recv()
        pbuf[i, h, xr, :, CA:BH] = (f(pbuf[i, h, xr, :, CA:BH]) + f(s_al[i])).astype(BF16)
        scatter(7, i).wait_recv()
        pbuf[i, h, xl, :, BH:CW] = (f(pbuf[i, h, xl, :, BH:CW]) + f(s_ar[i])).astype(BF16)
        scatter(8, i).start()
        scatter(9, i).start()

    def scatter3(b, n):
        i = b * NN + n
        scatter(4, i).wait_recv()
        rows = pl.ds(pl.multiple_of(b * 16, 16), 16)
        ca = pl.ds(pl.multiple_of(n * CW, 128), CA)
        cb = pl.ds(pl.multiple_of(n * CW + CA, 128), CW - CA)
        out_ref[rows, ca] = (
            f(pbuf[i, h, x, :, 0:CA]) + f(r_l[i, h]) + f(r_r[i, h]) + f(r_y[i])
        ).astype(BF16)
        scatter(8, i).wait_recv()
        scatter(9, i).wait_recv()
        out_ref[rows, cb] = (f(pbuf[i, h, x, :, CA:CW]) + f(s_l[i]) + f(s_r[i])).astype(BF16)

    def written(b, n):
        rows = pl.ds(pl.multiple_of(b * 16, 16), 16)
        cols = pl.ds(pl.multiple_of(n * CW, 128), CW)
        return pltpu.make_async_copy(out_ref.at[rows, cols], out_hbm.at[rows, cols], out_sem.at[b * NN + n])

    def first_step(s, carry):
        scatter0(0, s)
        return carry

    lax.fori_loop(0, NN, first_step, 0)
    cached(1, 0)
    cached(1, 1)
    fresh(1, 0)
    fresh(1, 1)

    @pl.when(c == 1)
    def _():
        decodes()

    scatter1(0)
    scatter1(1)

    def second_step(s, carry):
        @pl.when(s < NC)
        def _():
            scatter0(1, s - NN)

        @pl.when(s < NC + 2)
        def _():
            scatter1(s - 2)

        @pl.when(s < NC + 4)
        def _():
            scatter2(s - 4)

        @pl.when(s >= 6)
        def _():
            i = s - 6
            scatter3(i // NN, i % NN)
            written(i // NN, i % NN).start()

        return carry

    lax.fori_loop(NN, NC + 6, second_step, 0)

    def drain(i, carry):
        for k in range(17):
            gather(k, i).wait_send()
        for k in range(10):
            scatter(k, i).wait_send()
        return carry

    lax.fori_loop(0, NC, drain, 0)
    swap_pool.wait_send()
    swap_wo.wait_send()
    for i in range(NN):
        for b in range(NB):
            written(b, i).wait()
        swap_q(i).wait_send()
        swap_kv(i).wait_send()
    for b in range(NB):
        swap_new(b, 0).wait_send()
        swap_new(b, 1).wait_send()


def shards(x, gain, wq, wkv, wo, pool, table, offsets, lengths):
    half = np.arange(HD) % (HD // 2)
    freq = jnp.asarray((rope_base ** (-2.0 * half / HD)).astype(np.float32))[None]
    anyw = pl.BlockSpec(memory_space=pl.ANY)
    cb = CW - CA
    dma = pltpu.SemaphoreType.DMA
    return pl.pallas_call(
        kernel,
        name="block",
        out_shape=jax.ShapeDtypeStruct((32, D), BF16),
        in_specs=[anyw] * 10,
        out_specs=anyw,
        scratch_shapes=[
            pltpu.VMEM((32, D), BF16),
            pltpu.VMEM((32, D), BF16),
            pltpu.VMEM((1, D), F32),
            pltpu.VMEM((1, HD), F32),
            pltpu.SMEM((MAXP, 18), jnp.int32),
            pltpu.SMEM((2,), jnp.int32),
            pltpu.SMEM((16,), jnp.int32),
            pltpu.VMEM((NC, 128, CW), BF16),
            pltpu.VMEM((D, 768), BF16),
            pltpu.VMEM((512, D), BF16),
            pltpu.VMEM((16, PAGE, 2 * HD), BF16),
            pltpu.VMEM((2, SPAN, 2 * HD), BF16),
            pltpu.VMEM((NB, 128, 768), F32),
            pltpu.VMEM((512, 2 * HD), BF16),
            pltpu.VMEM((NB, 256, HD), BF16),
            pltpu.VMEM((NB, 320, HD), BF16),
            pltpu.VMEM((64, HD), BF16),
            pltpu.VMEM((2, NB, 128, HD), F32),
            pltpu.VMEM((320, SPAN), F32),
            pltpu.VMEM((320, 384), F32),
            pltpu.VMEM((64, 2048), F32),
            pltpu.VMEM((320, SPAN), BF16),
            pltpu.VMEM((64, 2048), BF16),
            pltpu.VMEM((NB, 2, 320, HD), F32),
            pltpu.VMEM((NB, 2, 320, HD), F32),
            pltpu.VMEM((NB, 2, 320, HD), F32),
            pltpu.VMEM((16, 2048), F32),
            pltpu.VMEM((NB, 128, 512), BF16),
            pltpu.VMEM((NC, 2, 4, 16, CW), BF16),
            pltpu.VMEM((NC, 2, 16, AH), BF16),
            pltpu.VMEM((NC, 2, 16, CA - AH), BF16),
            pltpu.VMEM((NC, 2, 16, CA), BF16),
            pltpu.VMEM((NC, 2, 16, CA), BF16),
            pltpu.VMEM((NC, 16, CA), BF16),
            pltpu.VMEM((NC, 4, 16, cb), BF16),
            pltpu.VMEM((NC, 16, BH - CA), BF16),
            pltpu.VMEM((NC, 16, CW - BH), BF16),
            pltpu.VMEM((NC, 16, cb), BF16),
            pltpu.VMEM((NC, 16, cb), BF16),
            dma((6,)),
            dma((NC,)),
            dma((4,)),
            dma((2 + 2 * NN,)),
            dma((2 + 2 * NN,)),
            dma((NC, 17)),
            dma((NC, 17)),
            dma((NB, 2)),
            dma((NB, 2)),
            dma((NC, 10)),
            dma((NC, 10)),
        ],
        compiler_params=pltpu.CompilerParams(
            collective_id=0, has_side_effects=True, vmem_limit_bytes=60 * 1024 * 1024
        ),
    )(x, gain[None], freq, wq, wkv, wo, pool, table.T, offsets, lengths)


def solution(mesh):
    placed = (
        P(("req", "tensor"), None),
        P(),
        P(None, "tensor"),
        P(None, "tensor"),
        P("tensor", None),
        P(("req", "tensor"), None, None),
        P("req", None),
        P("req"),
        P("req"),
    )
    return jax.shard_map(
        shards, mesh=mesh, in_specs=placed, out_specs=P(("req", "tensor"), None), check_vma=False
    )
```

```python
import functools

import jax
import jax.numpy as jnp
import numpy as np
from jax import lax
from jax.experimental import pallas as pl
from jax.experimental.pallas import tpu as pltpu
from jax.sharding import PartitionSpec as P

HD = 128
C = 248
PAGE = 128
MAXP = 8
ROWS = 512
D = 8192
CW = 2048
NN = D // CW
NB = 2
NC = NB * NN
CA = 1152
AH = 640
BH = CA + 384
eps_norm = 1e-06
rope_base = 1000000.0
neg_big = -1e30
MESH = pl.DeviceIdType.MESH
F32 = jnp.float32
BF16 = jnp.bfloat16
B_LO = (64, 48)
SPAN = MAXP * PAGE


def kernel(
    x_hbm, gain_hbm, freq_hbm, wq_hbm, wkv_hbm, wo_hbm, pool_hbm, table_hbm, off_hbm, len_hbm,
    out_hbm,
    out_ref, x_ref, gain_ref, freq_ref, table_ref, off_ref, len_ref, xg, w, wo, pool, kvc, acc, newkv, qa, qb, qd, trig, sc_ref, sf_ref, sd, pc, pd,
    m_ref, l_ref, o_ref, cnt, att, pbuf, r_al, r_ar, r_l, r_r, r_y, s_y, s_al, s_ar, s_l, s_r,
    in_sem, out_sem, own_sem, ws_sem, wr_sem, ag_s, ag_r, kv_s, kv_r, rs_s, rs_r,
):
    req = lax.axis_index("req")
    me = lax.axis_index("tensor")
    h, x, c = me // 8, (me // 2) % 4, me % 2

    def dev(hh, xx, cc):
        return (req, hh * 8 + xx * 2 + cc)

    xr, xl, xo = lax.rem(x + 1, 4), lax.rem(x + 3, 4), lax.rem(x + 2, 4)
    core_dev, right, left, across = dev(h, x, 1 - c), dev(h, xr, c), dev(h, xl, c), dev(1 - h, x, c)

    def send(src, dst, ssem, rsem, to):
        return pltpu.make_async_remote_copy(
            src_ref=src, dst_ref=dst, send_sem=ssem, recv_sem=rsem, device_id=to, device_id_type=MESH
        )

    barrier = pltpu.get_barrier_semaphore()
    for to in (core_dev, right, left, across):
        pl.semaphore_signal(barrier, inc=1, device_id=to, device_id_type=MESH)

    inputs = [
        pltpu.make_async_copy(src, dst, in_sem.at[k])
        for k, (src, dst) in enumerate(
            (
                (x_hbm, x_ref),
                (gain_hbm, gain_ref),
                (freq_hbm, freq_ref),
                (table_hbm, table_ref),
                (off_hbm, off_ref),
                (len_hbm, len_ref),
            )
        )
    ]
    for copy in inputs:
        copy.start()

    qcol = pl.multiple_of(c * 256, 256)
    kcol = pl.multiple_of(512 + c * 128, 128)
    orow = pl.multiple_of(c * 256, 256)
    prow = c * 8
    own = [
        pltpu.make_async_copy(pool_hbm, pool.at[pl.ds(prow, 8)], own_sem.at[0]),
        pltpu.make_async_copy(wq_hbm, w.at[:, pl.ds(qcol, 256)], own_sem.at[1]),
        pltpu.make_async_copy(wkv_hbm, w.at[:, pl.ds(kcol, 128)], own_sem.at[2]),
        pltpu.make_async_copy(wo_hbm, wo.at[pl.ds(orow, 256)], own_sem.at[3]),
    ]
    mine = pl.multiple_of((h * 4 + x) * 16, 16)
    total = jnp.zeros((32, 1), F32)
    inputs[0].wait()
    inputs[1].wait()
    for copy in own:
        copy.start()
    for i in range(NN):
        v = x_ref[:, i * CW : (i + 1) * CW].astype(F32)
        total = total + jnp.sum(v * v, axis=1, keepdims=True)
    inv = lax.rsqrt(total * (1.0 / D) + eps_norm)
    for i in range(NN):
        v = x_ref[:, i * CW : (i + 1) * CW].astype(F32)
        v = (v * inv * gain_ref[:, i * CW : (i + 1) * CW]).astype(BF16)
        for b in range(NB):
            xg[b * NN + i, pl.ds(mine, 16), :] = v[b * 16 : (b + 1) * 16]

    pl.semaphore_wait(barrier, 4)

    swap_pool = send(pool_hbm, pool.at[pl.ds(prow, 8)], ws_sem.at[0], wr_sem.at[0], core_dev)
    swap_wo = send(wo_hbm, wo.at[pl.ds(orow, 256)], ws_sem.at[1], wr_sem.at[1], core_dev)

    def swap_q(i):
        r = pl.ds(pl.multiple_of(i * CW, CW), CW)
        return send(wq_hbm.at[r], w.at[r, pl.ds(qcol, 256)], ws_sem.at[2 + i], wr_sem.at[2 + i], core_dev)

    def swap_kv(i):
        r = pl.ds(pl.multiple_of(i * CW, CW), CW)
        return send(
            wkv_hbm.at[r], w.at[r, pl.ds(kcol, 128)], ws_sem.at[2 + NN + i], wr_sem.at[2 + NN + i], core_dev
        )

    def block(hh, xx):
        return pl.multiple_of((hh * 4 + xx) * 16, 16)

    b_own, b_par = block(h, x), block(1 - h, x)
    b_l, b_r, b_o = block(h, xl), block(h, xr), block(h, xo)
    p_l, p_r = block(1 - h, xl), block(1 - h, xr)

    def gather(k, i):
        row, lo, hi, to = (
            (b_own, 0, CA, across),
            (b_own, 0, CA, right),
            (b_own, 0, CA, left),
            (b_par, 0, CA, right),
            (b_par, 0, CA, left),
            (b_l, 0, AH, right),
            (b_r, AH, CA, left),
            (p_l, 0, AH, right),
            (p_r, AH, CA, left),
            (b_own, CA, CW, right),
            (b_own, CA, CW, left),
            (b_own, CA, CW, across),
            (b_l, CA, BH, right),
            (b_r, BH, CW, left),
            (b_l, CA, CW, across),
            (b_r, CA, CW, across),
            (b_o, CA, CW, across),
        )[k]
        ref = xg.at[i, pl.ds(row, 16), lo:hi]
        return send(ref, ref, ag_s.at[i, k], ag_r.at[i, k], to)

    swap_pool.start()
    acc[...] = jnp.zeros_like(acc)

    def gather0(i):
        for k in (0, 1, 2, 9, 10, 11):
            gather(k, i).start()

    def gather1(i):
        gather(0, i).wait_recv()
        gather(3, i).start()
        gather(4, i).start()
        gather(9, i).wait_recv()
        gather(12, i).start()
        gather(14, i).start()
        gather(10, i).wait_recv()
        gather(13, i).start()
        gather(15, i).start()
        gather(1, i).wait_recv()
        gather(5, i).start()
        gather(2, i).wait_recv()
        gather(6, i).start()

    def gather2(i):
        gather(12, i).wait_recv()
        gather(13, i).wait_recv()
        gather(16, i).start()
        gather(3, i).wait_recv()
        gather(7, i).start()
        gather(4, i).wait_recv()
        gather(8, i).start()

    def arrived(i):
        for k in (5, 6, 7, 8, 11, 14, 15, 16):
            gather(k, i).wait_recv()

    def project(b, n, lo=0, hi=768):
        r = pl.ds(pl.multiple_of(n * CW, CW), CW)
        acc[b, :, lo:hi] += jnp.dot(xg[b * NN + n], w[r, lo:hi], preferred_element_type=F32)

    def gather_step(s, carry):
        @pl.when(s < NC)
        def _():
            gather0(s)

        @pl.when(s < NN)
        def _():
            swap_q(s).start()
            swap_kv(s).start()

        @pl.when(s >= 2)
        def _():
            gather1(s - 2)

        @pl.when(s >= 4)
        def _():
            gather2(s - 4)

        @pl.when(s == 4)
        def _():
            prepare()

        @pl.when(s >= 5)
        def _():
            n = s - 5
            swap_q(n).wait_recv()
            swap_kv(n).wait_recv()
            arrived(n)
            project(0, n)

        return carry

    def prepare():
        own[0].wait()
        own[1].wait()
        own[2].wait()
        for copy in inputs[2:]:
            copy.wait()
        swap_pool.wait_recv()
        swap_wo.start()
        for st in range(2):
            for j in range(MAXP):
                kvc[st, j * PAGE : (j + 1) * PAGE, :] = pool[table_ref[j, st]]
        slot = lax.broadcasted_iota(jnp.int32, (16, 2048), 1)
        page, inside = slot // PAGE, slot % PAGE
        rid = lax.broadcasted_iota(jnp.int32, (16, 1), 0)
        length = jnp.zeros((16, 1), jnp.int32)
        for b in range(16):
            length = jnp.where(rid == b, len_ref[b], length)
        count = jnp.zeros((16, 2048), F32)
        for j in range(MAXP):
            named = jnp.zeros((16, 1), jnp.int32)
            for b in range(16):
                named = jnp.where(rid == b, table_ref[j, 2 + b], named)
            seen = (page == named) & (inside + j * PAGE < length)
            count = count + jnp.where(seen, 1.0, 0.0)
        cnt[...] = count
        for b in range(NB):
            g = row_globals(b, lax.broadcasted_iota(jnp.int32, (128, 1), 0))
            position = jnp.where(g < C, off_ref[0] + g, off_ref[1] + g - C)
            for d in range(16):
                position = jnp.where(g == 2 * C + d, len_ref[d], position)
            angle = position.astype(F32) * freq_ref[...]
            lane = lax.broadcasted_iota(jnp.int32, (128, HD), 1)
            trig[0, b] = jnp.cos(angle)
            trig[1, b] = jnp.where(lane < HD // 2, -jnp.sin(angle), jnp.sin(angle))

    def row_globals(b, lr):
        return ((lr // 16) * 2 + c) * 32 + b * 16 + lr % 16

    def key_globals(row):
        j = row // 256 * 4 + row % 64 // 16
        return (j * 2 + row // 128 % 2) * 32 + row // 64 % 2 * 16 + row % 16

    def rotated(b, col):
        v = acc[b, :, col : col + HD]
        return (v * trig[0, b] + pltpu.roll(v, HD // 2, 1) * trig[1, b]).astype(BF16)

    def swap_new(b, half):
        ref = newkv.at[pl.ds(pl.multiple_of(half * 256 + c * 128 + b * 64, 64), 64)]
        return send(ref, ref, kv_s.at[b, half], kv_r.at[b, half], core_dev)

    def head_rows(b, n):
        lo = B_LO[b]
        return slice(n * (128 - lo), (n + 1) * (128 - lo))

    def place_new(b):
        k = rotated(b, 512)
        v = acc[b, :, 640:768].astype(BF16)
        for half in range(2):
            rows = pl.ds(pl.multiple_of(half * 256 + c * 128 + b * 64, 64), 64)
            newkv[rows, 0:HD] = k[half * 64 : (half + 1) * 64]
            newkv[rows, HD : 2 * HD] = v[half * 64 : (half + 1) * 64]

    def place_queries(b):
        for n in range(4):
            q = rotated(b, n * HD)
            qa[b, n * 64 : (n + 1) * 64, :] = q[0:64]
            qb[b, head_rows(b, n), :] = q[B_LO[b] : 128]
            if b == 1:
                qd[n * 16 : (n + 1) * 16, :] = q[112:128]

    def exchange(b):
        swap_new(b, 0).start()
        swap_new(b, 1).start()

    def nt(a, b):
        return lax.dot_general(a, b, (((1,), (1,)), ((), ())), preferred_element_type=F32)

    scale = HD ** (-0.5)

    def queries(b, st):
        return qa[b] if st == 0 else qb[b, 0 : 4 * (128 - B_LO[b]), :]

    def cached(b, st):
        q = queries(b, st)
        n = q.shape[0]
        sc_ref[0:n, :] = nt(q, kvc[st, :, 0:HD])
        slots = lax.broadcasted_iota(jnp.int32, (1, SPAN), 1)
        limit = off_ref[st]

        def some(k, carry):
            rows = pl.ds(pl.multiple_of(k * 32, 32), 32)
            v = jnp.where(slots < limit, sc_ref[rows, :], neg_big)
            m = jnp.max(v, axis=1, keepdims=True)
            e = jnp.exp((v - m) * scale)
            m_ref[b, st, rows, :] = jnp.broadcast_to(m, (32, HD))
            l_ref[b, st, rows, :] = jnp.broadcast_to(jnp.sum(e, axis=1, keepdims=True), (32, HD))
            pc[rows, :] = e.astype(BF16)
            return carry

        lax.fori_loop(0, n // 32, some, 0, unroll=True)
        o_ref[b, st, 0:n, :] = jnp.dot(pc[0:n, :], kvc[st, :, HD : 2 * HD], preferred_element_type=F32)

    def fresh(b, st):
        q = queries(b, st)
        k0, width = (0, 256) if st == 0 else (128, 384)
        n = q.shape[0] // 4
        sf_ref[0 : 4 * n, 0:width] = nt(q, newkv[k0 : k0 + width, 0:HD])
        lo = 0 if st == 0 else B_LO[b]
        kg = key_globals(k0 + lax.broadcasted_iota(jnp.int32, (1, width), 1))
        qg = row_globals(b, lo + lax.broadcasted_iota(jnp.int32, (n, 1), 0))
        seen = (kg <= qg) & (kg < C if st == 0 else kg >= C)
        for head in range(4):
            rows = slice(head * n, (head + 1) * n)
            v = jnp.where(seen, sf_ref[rows, 0:width], neg_big)
            m1 = m_ref[b, st, rows, :]
            m = jnp.maximum(m1, jnp.max(v, axis=1, keepdims=True))
            alpha = jnp.exp((m1 - m) * scale)
            e = jnp.exp((v - m[:, 0:1]) * scale)
            tot = alpha * l_ref[b, st, rows, :] + jnp.sum(e, axis=1, keepdims=True)
            o = jnp.dot(e.astype(BF16), newkv[k0 : k0 + width, HD : 2 * HD], preferred_element_type=F32)
            o = ((alpha * o_ref[b, st, rows, :] + o) / tot).astype(BF16)
            cols = slice(head * HD, (head + 1) * HD)
            if st == 0:
                att[b, 0:64, cols] = o
            elif b == 0:
                att[b, 64:128, cols] = o
            else:
                near = lax.broadcasted_iota(jnp.int32, (16, 1), 0) >= 8 + 8 * (1 - c)
                att[b, 64:128, cols] = o[16:]
                att[b, 48:64, cols] = jnp.where(
                    near, o[0:16].astype(F32), att[b, 48:64, cols].astype(F32)
                ).astype(BF16)

    def decodes():
        for b in range(16):
            sd[:, b * 128 : (b + 1) * 128] = nt(qd[...], pool[b, :, 0:HD])
        self_s = nt(qd[...], newkv[496:512, 0:HD])
        kid = lax.broadcasted_iota(jnp.int32, (64, 16), 1)
        qid = lax.broadcasted_iota(jnp.int32, (64, 16), 0) % 16
        self_s = jnp.where(kid == qid, self_s, neg_big)
        for n in range(4):
            rows = slice(n * 16, (n + 1) * 16)
            own_s = self_s[n * 16 : (n + 1) * 16]
            count = cnt[...]
            v = jnp.where(count > 0.0, sd[rows, :], neg_big)
            m = jnp.maximum(jnp.max(v, axis=1, keepdims=True), jnp.max(own_s, axis=1, keepdims=True))
            e = count * jnp.exp((v - m) * scale)
            e_own = jnp.exp((own_s - m) * scale)
            tot = jnp.sum(e, axis=1, keepdims=True) + jnp.sum(e_own, axis=1, keepdims=True)
            pd[rows, :] = e.astype(BF16)
            o = jnp.dot(e_own.astype(BF16), newkv[496:512, HD : 2 * HD], preferred_element_type=F32)
            for b in range(16):
                o = o + jnp.dot(
                    pd[rows, b * 128 : (b + 1) * 128], pool[b, :, HD : 2 * HD], preferred_element_type=F32
                )
            sd[rows, 0:HD] = o / tot

    lax.fori_loop(0, NC + 1, gather_step, 0)
    gather1(7)
    gather2(5)
    place_new(0)
    place_queries(0)
    exchange(0)
    cached(0, 0)
    gather2(6)
    cached(0, 1)
    gather2(7)
    arrived(4)
    project(1, 0)
    arrived(5)
    project(1, 1)
    arrived(6)
    project(1, 2)
    arrived(7)
    project(1, 3, 512, 768)
    place_new(1)
    project(1, 3, 0, 256)
    exchange(1)
    project(1, 3, 256, 512)
    place_queries(1)

    @pl.when(c == 1)
    def _():
        decodes()

    for b in range(NB):
        swap_new(b, 0).wait_recv()
        swap_new(b, 1).wait_recv()
    fresh(0, 0)
    fresh(0, 1)
    own[3].wait()
    swap_wo.wait_recv()

    def scatter(k, i):
        ss, rr = rs_s.at[i, k], rs_r.at[i, k]
        if k == 0:
            return send(pbuf.at[i, :, xo, :, 0:AH], r_al.at[i], ss, rr, right)
        if k == 1:
            return send(pbuf.at[i, :, xo, :, AH:CA], r_ar.at[i], ss, rr, left)
        if k == 2:
            return send(pbuf.at[i, :, xr, :, 0:CA], r_l.at[i], ss, rr, right)
        if k == 3:
            return send(pbuf.at[i, :, xl, :, 0:CA], r_r.at[i], ss, rr, left)
        if k == 4:
            return send(pbuf.at[i, 1 - h, x, :, 0:CA], r_y.at[i], ss, rr, across)
        if k == 5:
            return send(pbuf.at[i, 1 - h, :, :, CA:CW], s_y.at[i], ss, rr, across)
        if k == 6:
            return send(pbuf.at[i, h, xo, :, CA:BH], s_al.at[i], ss, rr, right)
        if k == 7:
            return send(pbuf.at[i, h, xo, :, BH:CW], s_ar.at[i], ss, rr, left)
        if k == 8:
            return send(pbuf.at[i, h, xr, :, CA:CW], s_l.at[i], ss, rr, right)
        return send(pbuf.at[i, h, xl, :, CA:CW], s_r.at[i], ss, rr, left)

    def f(v):
        return v.astype(F32)

    def scatter0(b, n):
        i = b * NN + n
        for k in range(CW // 256):
            col = pl.multiple_of(n * CW + k * 256, 256)
            prod = jnp.dot(att[b], wo[:, pl.ds(col, 256)], preferred_element_type=F32)
            pbuf[i, :, :, :, k * 256 : (k + 1) * 256] = prod.astype(BF16).reshape(2, 4, 16, 256)
        for k in (0, 1, 5):
            scatter(k, i).start()

    def scatter1(i):
        scatter(0, i).wait_recv()
        pbuf[i, :, xr, :, 0:AH] = (f(pbuf[i, :, xr, :, 0:AH]) + f(r_al[i])).astype(BF16)
        scatter(1, i).wait_recv()
        pbuf[i, :, xl, :, AH:CA] = (f(pbuf[i, :, xl, :, AH:CA]) + f(r_ar[i])).astype(BF16)
        scatter(2, i).start()
        scatter(3, i).start()
        scatter(5, i).wait_recv()
        pbuf[i, h, :, :, CA:CW] = (f(pbuf[i, h, :, :, CA:CW]) + f(s_y[i])).astype(BF16)
        scatter(6, i).start()
        scatter(7, i).start()

    def scatter2(i):
        scatter(2, i).wait_recv()
        scatter(3, i).wait_recv()
        pbuf[i, 1 - h, x, :, 0:CA] = (
            f(pbuf[i, 1 - h, x, :, 0:CA]) + f(r_l[i, 1 - h]) + f(r_r[i, 1 - h])
        ).astype(BF16)
        scatter(4, i).start()
        scatter(6, i).wait_recv()
        pbuf[i, h, xr, :, CA:BH] = (f(pbuf[i, h, xr, :, CA:BH]) + f(s_al[i])).astype(BF16)
        scatter(7, i).wait_recv()
        pbuf[i, h, xl, :, BH:CW] = (f(pbuf[i, h, xl, :, BH:CW]) + f(s_ar[i])).astype(BF16)
        scatter(8, i).start()
        scatter(9, i).start()

    def scatter3(b, n):
        i = b * NN + n
        scatter(4, i).wait_recv()
        rows = pl.ds(pl.multiple_of(b * 16, 16), 16)
        ca = pl.ds(pl.multiple_of(n * CW, 128), CA)
        cb = pl.ds(pl.multiple_of(n * CW + CA, 128), CW - CA)
        out_ref[rows, ca] = (
            f(pbuf[i, h, x, :, 0:CA]) + f(r_l[i, h]) + f(r_r[i, h]) + f(r_y[i])
        ).astype(BF16)
        scatter(8, i).wait_recv()
        scatter(9, i).wait_recv()
        out_ref[rows, cb] = (f(pbuf[i, h, x, :, CA:CW]) + f(s_l[i]) + f(s_r[i])).astype(BF16)

    def written(b, n):
        rows = pl.ds(pl.multiple_of(b * 16, 16), 16)
        cols = pl.ds(pl.multiple_of(n * CW, 128), CW)
        return pltpu.make_async_copy(out_ref.at[rows, cols], out_hbm.at[rows, cols], out_sem.at[b * NN + n])

    def first_step(s, carry):
        scatter0(0, s)
        return carry

    lax.fori_loop(0, NN, first_step, 0)
    cached(1, 0)
    cached(1, 1)
    fresh(1, 0)
    fresh(1, 1)

    @pl.when(c == 1)
    def _():
        for n in range(4):
            att[1, 112:128, n * HD : (n + 1) * HD] = sd[n * 16 : (n + 1) * 16, 0:HD].astype(BF16)

    scatter1(0)
    scatter1(1)

    def second_step(s, carry):
        @pl.when(s < NC)
        def _():
            scatter0(1, s - NN)

        @pl.when(s < NC + 2)
        def _():
            scatter1(s - 2)

        @pl.when(s < NC + 4)
        def _():
            scatter2(s - 4)

        @pl.when(s >= 6)
        def _():
            i = s - 6
            scatter3(i // NN, i % NN)
            written(i // NN, i % NN).start()

        return carry

    lax.fori_loop(NN, NC + 6, second_step, 0)

    def drain(i, carry):
        for k in range(17):
            gather(k, i).wait_send()
        for k in range(10):
            scatter(k, i).wait_send()
        return carry

    lax.fori_loop(0, NC, drain, 0)
    swap_pool.wait_send()
    swap_wo.wait_send()
    for i in range(NN):
        for b in range(NB):
            written(b, i).wait()
        swap_q(i).wait_send()
        swap_kv(i).wait_send()
    for b in range(NB):
        swap_new(b, 0).wait_send()
        swap_new(b, 1).wait_send()


def shards(x, gain, wq, wkv, wo, pool, table, offsets, lengths):
    half = np.arange(HD) % (HD // 2)
    freq = jnp.asarray((rope_base ** (-2.0 * half / HD)).astype(np.float32))[None]
    anyw = pl.BlockSpec(memory_space=pl.ANY)
    cb = CW - CA
    dma = pltpu.SemaphoreType.DMA
    return pl.pallas_call(
        kernel,
        name="block",
        out_shape=jax.ShapeDtypeStruct((32, D), BF16),
        in_specs=[anyw] * 10,
        out_specs=anyw,
        scratch_shapes=[
            pltpu.VMEM((32, D), BF16),
            pltpu.VMEM((32, D), BF16),
            pltpu.VMEM((1, D), F32),
            pltpu.VMEM((1, HD), F32),
            pltpu.SMEM((MAXP, 18), jnp.int32),
            pltpu.SMEM((2,), jnp.int32),
            pltpu.SMEM((16,), jnp.int32),
            pltpu.VMEM((NC, 128, CW), BF16),
            pltpu.VMEM((D, 768), BF16),
            pltpu.VMEM((512, D), BF16),
            pltpu.VMEM((16, PAGE, 2 * HD), BF16),
            pltpu.VMEM((2, SPAN, 2 * HD), BF16),
            pltpu.VMEM((NB, 128, 768), F32),
            pltpu.VMEM((512, 2 * HD), BF16),
            pltpu.VMEM((NB, 256, HD), BF16),
            pltpu.VMEM((NB, 320, HD), BF16),
            pltpu.VMEM((64, HD), BF16),
            pltpu.VMEM((2, NB, 128, HD), F32),
            pltpu.VMEM((320, SPAN), F32),
            pltpu.VMEM((320, 384), F32),
            pltpu.VMEM((64, 2048), F32),
            pltpu.VMEM((320, SPAN), BF16),
            pltpu.VMEM((64, 2048), BF16),
            pltpu.VMEM((NB, 2, 320, HD), F32),
            pltpu.VMEM((NB, 2, 320, HD), F32),
            pltpu.VMEM((NB, 2, 320, HD), F32),
            pltpu.VMEM((16, 2048), F32),
            pltpu.VMEM((NB, 128, 512), BF16),
            pltpu.VMEM((NC, 2, 4, 16, CW), BF16),
            pltpu.VMEM((NC, 2, 16, AH), BF16),
            pltpu.VMEM((NC, 2, 16, CA - AH), BF16),
            pltpu.VMEM((NC, 2, 16, CA), BF16),
            pltpu.VMEM((NC, 2, 16, CA), BF16),
            pltpu.VMEM((NC, 16, CA), BF16),
            pltpu.VMEM((NC, 4, 16, cb), BF16),
            pltpu.VMEM((NC, 16, BH - CA), BF16),
            pltpu.VMEM((NC, 16, CW - BH), BF16),
            pltpu.VMEM((NC, 16, cb), BF16),
            pltpu.VMEM((NC, 16, cb), BF16),
            dma((6,)),
            dma((NC,)),
            dma((4,)),
            dma((2 + 2 * NN,)),
            dma((2 + 2 * NN,)),
            dma((NC, 17)),
            dma((NC, 17)),
            dma((NB, 2)),
            dma((NB, 2)),
            dma((NC, 10)),
            dma((NC, 10)),
        ],
        compiler_params=pltpu.CompilerParams(
            collective_id=0, has_side_effects=True, vmem_limit_bytes=60 * 1024 * 1024
        ),
    )(x, gain[None], freq, wq, wkv, wo, pool, table.T, offsets, lengths)


def solution(mesh):
    placed = (
        P(("req", "tensor"), None),
        P(),
        P(None, "tensor"),
        P(None, "tensor"),
        P("tensor", None),
        P(("req", "tensor"), None, None),
        P("req", None),
        P("req"),
        P("req"),
    )
    return jax.shard_map(
        shards, mesh=mesh, in_specs=placed, out_specs=P(("req", "tensor"), None), check_vma=False
    )
```
